256 devices in a mesh: gx: 4 (over y), gy: 4 (over z_hi, core), gz: 16 (over x, z_lo).
Axes of the slice: x: 4, y: 4, z: 8 (z_hi: 2, z_lo: 4; z = z_hi * 4 + z_lo), core: 2. Of those that a mesh axis runs over, the one named last changes fastest.
Arguments:
- concentration: float32 [192, 64, 2048], P('gx', 'gy', 'gz'), may hold values from -6 to 6
- dispersion: float32 [192, 64, 2048], P('gx', 'gy', 'gz'), may hold values from 0.2 to 1.2
- disp_step: float32 [192, 64, 2048], P('gx', 'gy', 'gz'), may hold values from -6 to 6
- capacity: float32 [192, 64, 2048], P('gx', 'gy', 'gz'), may hold values from 1 to 4
- cap_step: float32 [192, 64, 2048], P('gx', 'gy', 'gz'), may hold values from -6 to 6
- velocity: float32 [192, 64, 2048], P('gx', 'gy', 'gz'), may hold values from 0.2 to 1
- voxel_mask: int32 [24, 8, 256], P('gx', 'gy', 'gz'), may hold values 0 or 1
- voxel_class: int32 [24, 8, 256], P('gx', 'gy', 'gz'), may hold values from 0 to 3
- class_weight: float32 [4], replicated, may hold values from 4 to 40
Outputs:
- grad_dispersion: float32 [192, 64, 2048], P('gx', 'gy', 'gz')
- grad_capacity: float32 [192, 64, 2048], P('gx', 'gy', 'gz')
The draws below stay inside these ranges and needn't reach their ends.
All inputs are finite; a program needn't handle non-finite values. No bound on the sum of `voxel_mask` on one device may be relied on, other than what follows from the above.
Results may differ from the reference program's by a relative error of at most 0.00024.
Values sent between devices are 32-bit elements; how exact they have to be, the bound alone decides.
No kernel may reach another device: no remote copies, remote signals or barrier semaphores. Data moves between devices by JAX's collectives and lax.ppermute only.
A program may use at most 64 MiB of HBM per device.

```python
import math
import jax
import jax.numpy as jnp
from jax import lax

CLASSES = 4
NX = 192
NY = 64
NZ = 2048
MX = 24
MY = 8
MZ = 256


def set_ends(drawn, rng, least, largest):
    dims = drawn.shape
    spot = [jax.random.randint(jax.random.fold_in(rng, axis), (), 0, dims[axis]) for axis in range(len(dims))]
    drawn = drawn.at[tuple(spot)].set(least)
    longest = dims.index(max(dims))
    spot[longest] = (spot[longest] + 1) % dims[longest]
    return drawn.at[tuple(spot)].set(largest)


def steps_of(own_key, dims, split, low, largest):
    level = 1.0
    for position, blocks in split:
        heights = jax.random.uniform(jax.random.fold_in(jax.random.fold_in(own_key, 6), position), (blocks,), jnp.float32, low / len(split), largest / len(split))
        level = level * jnp.repeat(jnp.exp(heights), dims[position] // blocks).reshape((-1,) + (1,) * (len(dims) - 1 - position))
    return level


def centred(own_key, extent, deviation, limit, shards=(), held_as=jnp.bfloat16):
    values = jax.random.normal(own_key, extent, jnp.float32) * deviation
    if len(shards) > 0:
        values = steps_of(own_key, extent, shards, -0.22, 0.18) * values
    return jnp.clip(values, min=-limit, max=limit).astype(held_as)


def setup_inputs(seed: int = 0) -> dict:
    arg_keys = jax.random.split(jax.random.key(seed), 10)
    return {
        "concentration": centred(arg_keys[0], (NX, NY, NZ), 1.0, 6.0, ((0, 4), (1, 4), (2, 16)), jnp.float32),
        "dispersion": jnp.clip(0.2 + 1 * jax.random.uniform(arg_keys[1], (NX, NY, NZ), jnp.float32) ** steps_of(arg_keys[1], (NX, NY, NZ), ((0, 4), (1, 4), (2, 16)), -0.2, 0.2), 0.2, 1.2),
        "disp_step": centred(arg_keys[2], (NX, NY, NZ), 1.0, 6.0, ((0, 4), (1, 4), (2, 16)), jnp.float32),
        "capacity": jnp.clip(1.0 + 3.0 * jax.random.uniform(arg_keys[3], (NX, NY, NZ), jnp.float32) ** steps_of(arg_keys[3], (NX, NY, NZ), ((0, 4), (1, 4), (2, 16)), -0.2, 0.2), 1.0, 4.0),
        "cap_step": centred(arg_keys[4], (NX, NY, NZ), 1.0, 6.0, ((0, 4), (1, 4), (2, 16)), jnp.float32),
        "velocity": jnp.clip(0.2 + 0.8 * jax.random.uniform(arg_keys[5], (NX, NY, NZ), jnp.float32) ** steps_of(arg_keys[5], (NX, NY, NZ), ((0, 4), (1, 4), (2, 16)), -0.2, 0.2), 0.2, 1.0),
        "voxel_mask": set_ends((jax.random.randint(arg_keys[6], (MX, MY, MZ), 0, 4) < 3).astype(jnp.int32), jax.random.fold_in(arg_keys[6], 1), 0, 1),
        "voxel_class": set_ends(jax.random.randint(arg_keys[7], (MX, MY, MZ), 0, CLASSES), jax.random.fold_in(arg_keys[7], 1), 0, CLASSES - 1).astype(jnp.int32),
        "class_weight": jnp.clip(jnp.exp(jax.random.uniform(arg_keys[8], (CLASSES,), jnp.float32, math.log(4.0), math.log(40.0))), 4.0, 40.0),
    }


time_step = 0.1

def sides(padded):
    return [padded[2:, 1:-1, 1:-1], padded[:-2, 1:-1, 1:-1], padded[1:-1, 2:, 1:-1], padded[1:-1, :-2, 1:-1], padded[1:-1, 1:-1, 2:], padded[1:-1, 1:-1, :-2]]

def inner(padded):
    return padded[1:-1, 1:-1, 1:-1]

def diffuse(field_pad, coef_pad):
    center = inner(field_pad)
    coef = inner(coef_pad)
    total = jnp.zeros(center.shape, jnp.float32)
    for near_field, near_coef in zip(sides(field_pad), sides(coef_pad)):
        total = total + 0.5 * (coef + near_coef) * (near_field - center)
    return total

def advect(field_pad, vel_pad):
    return vel_pad[1:-1, 1:-1, :-2] * field_pad[1:-1, 1:-1, :-2] - inner(vel_pad) * inner(field_pad)

def advect_back(field_pad, vel_center):
    return vel_center * (field_pad[1:-1, 1:-1, 2:] - inner(field_pad))

def face_grad(mult_pad, field_pad):
    mult = inner(mult_pad)
    center = inner(field_pad)
    total = jnp.zeros(center.shape, jnp.float32)
    for near_mult, near_field in zip(sides(mult_pad), sides(field_pad)):
        total = total + 0.5 * (mult - near_mult) * (near_field - center)
    return total

def voxel_weights(voxel_mask, voxel_class, class_weight):
    labels = jnp.arange(class_weight.shape[0]).astype(jnp.int32)
    picked = jnp.where(voxel_class[None] == labels[:, None, None, None], class_weight[:, None, None, None], 0.0)
    return voxel_mask.astype(jnp.float32) * lax.optimization_barrier(jnp.sum(picked, axis=0))

def restrict_prolong(final, weights):
    sx, sy, sz = weights.shape
    coarse = final.reshape(sx, 8, sy, 8, sz, 8).mean(axis=(1, 3, 5))
    valued = weights * coarse
    return jnp.broadcast_to(valued[:, None, :, None, :, None], (sx, 8, sy, 8, sz, 8)).reshape(final.shape)

def reference(concentration, dispersion, disp_step, capacity, cap_step, velocity, voxel_mask, voxel_class, class_weight):
    conc_pad = jnp.pad(concentration, 1)
    disp_pad = jnp.pad(dispersion, 1)
    step_pad = jnp.pad(disp_step, 1)
    vel_pad = jnp.pad(velocity, 1)
    first_rate = diffuse(conc_pad, disp_pad) + advect(conc_pad, vel_pad)
    later = concentration + time_step / capacity * first_rate
    tangent = time_step / capacity * diffuse(conc_pad, step_pad) - time_step * cap_step / capacity ** 2 * first_rate
    later_pad = jnp.pad(later, 1)
    tangent_pad = jnp.pad(tangent, 1)
    second_rate = diffuse(later_pad, disp_pad) + advect(later_pad, vel_pad)
    final = tangent + time_step / capacity * (diffuse(tangent_pad, disp_pad) + advect(tangent_pad, vel_pad) + diffuse(later_pad, step_pad)) - time_step * cap_step / capacity ** 2 * second_rate
    weights = voxel_weights(voxel_mask, voxel_class, class_weight)
    source = restrict_prolong(final, weights)
    scaled = time_step * source / capacity
    scaled_pad = jnp.pad(scaled, 1)
    earlier = source + diffuse(scaled_pad, disp_pad) + advect_back(scaled_pad, velocity)
    scaled_first = time_step * earlier / capacity
    first_pad = jnp.pad(scaled_first, 1)
    grad_dispersion = face_grad(scaled_pad, later_pad) + face_grad(first_pad, conc_pad)
    grad_capacity = -scaled * second_rate / capacity - scaled_first * first_rate / capacity
    return (grad_dispersion, grad_capacity)
```

```python
import jax
import jax.numpy as jnp
from jax import lax
from jax.experimental import pallas as pl
from jax.experimental.pallas import tpu as pltpu
from jax.sharding import PartitionSpec as P

DT = 0.1
F32 = jnp.float32
VM = pl.BlockSpec(memory_space=pltpu.VMEM)
SM = pl.BlockSpec(memory_space=pltpu.SMEM)
HB = pl.BlockSpec(memory_space=pl.ANY)


def swap_pairs(size, first):
    pairs = []
    for i in range(first, size - 1, 2):
        pairs += [(i, i + 1), (i + 1, i)]
    return pairs


def swap(value, axis, first):
    return lax.ppermute(value, axis, swap_pairs(lax.axis_size(axis), first))


def call(body, outs, specs, args, scratch=(), limit=24):
    return pl.pallas_call(
        body,
        out_shape=[jax.ShapeDtypeStruct(s, F32) for s in outs],
        in_specs=specs,
        out_specs=[VM] * len(outs),
        scratch_shapes=list(scratch),
        compiler_params=pltpu.CompilerParams(vmem_limit_bytes=limit << 20),
    )(*args)


def rows(shape):
    return lax.broadcasted_iota(jnp.int32, shape, len(shape) - 2)


def lanes(shape):
    return lax.broadcasted_iota(jnp.int32, shape, len(shape) - 1)


def up(x, axis):
    return pltpu.roll(x, x.shape[axis] - 1, axis)


def down(x, axis):
    return pltpu.roll(x, 1, axis)


def rolled(x, shift, axis):
    shift = shift % x.shape[axis]
    return x if shift == 0 else pltpu.roll(x, shift, axis)


def pack_x(idx, c, d, s, cap, m, v, b0, b1, sems):
    n = c.shape[0]
    even = idx[0] == 0
    copies = []
    for out, hi in ((b0, even), (b1, jnp.logical_not(even))):
        one = jnp.where(hi, n - 1, 0)
        two = jnp.where(hi, n - 2, 1)
        for slot, (ref, at) in enumerate(
            [(r, i) for r in (c, d, s, cap) for i in (one, two)] + [(m, one), (v, one)]
        ):
            copies.append(pltpu.make_async_copy(ref.at[at], out.at[slot], sems.at[len(copies)]))
    for copy in copies:
        copy.start()
    for copy in copies:
        copy.wait()


def pack_y(idx, c, d, s, cap, m, v, rx0, rx1, b0, b1):
    n = c.shape[0]
    xeven = idx[0] == 0
    yeven = idx[1] == 0
    row = rows((8, 128))

    def tiles(four, low):
        out = None
        for f, value in enumerate(four):
            part = rolled(value, 2 * f if low else 2 * f + 2, 0)
            out = part if f == 0 else jnp.where(row < 2 * f, out, part)
        return out

    def put(at, lo, hi):
        b0[at] = jnp.where(yeven, hi, lo)
        b1[at] = jnp.where(yeven, lo, hi)

    def plane(x, _):
        lo = tiles([r[x, 0:8, :] for r in (c, d, s, cap)], True)
        hi = tiles([r[x, 8:16, :] for r in (c, d, s, cap)], False)
        put(x + 1, lo, hi)
        return 0

    lax.fori_loop(0, n, plane, 0, unroll=4)
    for at, pick in ((0, xeven), (n + 1, jnp.logical_not(xeven))):
        four = [jnp.where(pick, rx1[k], rx0[k]) for k in (0, 2, 4, 6)]
        put(at, tiles([q[0:8] for q in four], True), tiles([q[8:16] for q in four], False))

    def group(g, _):
        lo = hi = None
        for k in range(8):
            ref = (m, v)[k % 2]
            x = g * 4 + k // 2
            a = rolled(ref[x, 0:8, :], k, 0)
            b = rolled(ref[x, 8:16, :], k + 1, 0)
            lo = a if k == 0 else jnp.where(row < k, lo, a)
            hi = b if k == 0 else jnp.where(row < k, hi, b)
        put(n + 2 + g, lo, hi)
        return 0

    lax.fori_loop(0, n // 4, group, 0)


def pack_z(idx, c, d, s, cap, m, v, rx0, rx1, ry0, ry1, p, t):
    n = c.shape[0]
    xeven = idx[0] == 0
    yeven = idx[1] == 0
    row = rows((8, 128))
    zero = jnp.zeros((8, 128), F32)
    fields = (c, d, s, cap, m, v)

    def both(at):
        one, two = (ry0[at], ry1[at])
        return jnp.where(yeven, one, two), jnp.where(yeven, two, one)

    def third(hi, lo, f):
        return jnp.where(row < 4, rolled(hi, -2 * f, 0), rolled(lo, 6 - 2 * f, 0))

    def group(g, _):
        mvhi, mvlo = both(n + 2 + g)
        for k in range(4):
            x = g * 4 + k
            hi, lo = both(x + 1)
            for f in range(6):
                p[f, x + 2, 0:16, :] = fields[f][x]
                if f < 4:
                    p[f, x + 2, 16:24, :] = third(hi, lo, f)
                else:
                    r = 2 * k + f - 4
                    p[f, x + 2, 16:24, :] = jnp.where(
                        row < 4, rolled(mvhi, -r, 0), rolled(mvlo, 7 - r, 0)
                    )
        return 0

    lax.fori_loop(0, n // 4, group, 0)
    for near, far, at, pick in (
        (1, 0, 0, xeven),
        (n + 2, n + 3, n + 1, jnp.logical_not(xeven)),
    ):
        hi, lo = both(at)
        for f in range(6):
            slot = 2 * f if f < 4 else 4 + f
            p[f, near, 0:16, :] = jnp.where(pick, rx1[slot], rx0[slot])
            p[f, near, 16:24, :] = third(hi, lo, f) if f < 4 else zero
            p[f, far, 0:16, :] = (
                jnp.where(pick, rx1[slot + 1], rx0[slot + 1]) if f < 4 else jnp.zeros((16, 128), F32)
            )
            p[f, far, 16:24, :] = zero
    lane = lanes((24, 128))

    def pack(g, _):
        out = None
        for k in range(30):
            part = rolled(p[k % 6, g * 5 + k // 6 + 1], 4 * k + 2, 1)
            out = part if k == 0 else jnp.where(lane < 4 * k, out, part)
        t[g] = out
        return 0

    lax.fori_loop(0, (n + 2) // 5, pack, 0)


def face_sum(flux_x, flux_xm, flux_y, flux_z):
    return (flux_x - flux_xm) + (flux_y - down(flux_y, 0)) + (flux_z - down(flux_z, 1))


def forward(idx, cw, p, rz0, rz1, mask, cls, v_out, h, a_out, later, r1, r2, tang, q_s, hs, cs):
    n = r1.shape[0]
    zeven = idx[2] == 0
    lane = lanes((24, 128))

    def unpack(g, _):
        one, two = (rz0[g], rz1[g])
        hi = jnp.where(zeven, one, two)
        lo = jnp.where(zeven, two, one)
        both = jnp.where(lane % 4 < 2, lo, hi)
        for k in range(30):
            part = rolled(both, -(4 * k + 2), 1)
            f, e = (k % 6, g * 5 + k // 6 + 1)
            if f in (0, 1, 5):
                h[(0, 1, None, None, None, 2)[f], e] = part
            else:
                hs[f - 2, e] = part
        return 0

    lax.fori_loop(0, (n + 2) // 5, unpack, 0)
    for e in (0, n + 3):
        for k in range(3):
            h[k, e] = jnp.zeros((24, 128), F32)
            hs[k, e] = jnp.zeros((24, 128), F32)

    def load(f, e):
        halo = h[(0, 1, None, None, None, 2)[f], e] if f in (0, 1, 5) else hs[f - 2, e]
        return jnp.concatenate([p[f, e], halo], axis=1)

    def inverse(e):
        cap = load(3, e)
        a_out[e] = DT * jnp.where(cap > 0, 1.0 / jnp.where(cap > 0, cap, 1.0), 0.0)

    def make(e, _):
        inverse(e)
        return 0

    lax.fori_loop(0, n + 4, make, 0)

    def first(t, carry):
        c0, d0, s0, fd, fs = carry
        e = t + 1
        c1, d1, s1 = (load(0, e + 1), load(1, e + 1), load(2, e + 1))
        gx = c1 - c0
        fdx = (d0 + d1) * gx
        fsx = (s0 + s1) * gx
        gy = up(c0, 0) - c0
        fdy = (d0 + up(d0, 0)) * gy
        fsy = (s0 + up(s0, 0)) * gy
        gz = up(c0, 1) - c0
        fdz = (d0 + up(d0, 1)) * gz
        fsz = (s0 + up(s0, 1)) * gz
        vc = load(5, e) * c0
        rate = 0.5 * face_sum(fdx, fd, fdy, fdz) + (down(vc, 1) - vc)
        a = a_out[e]
        q = (1 / DT) * a * load(4, e)
        later[t] = c0 + a * rate
        tang[t] = a * (0.5 * face_sum(fsx, fs, fsy, fsz) - q * rate)
        q_s[t] = q[0:16, 0:128]
        r1[jnp.clip(t - 1, 0, n - 1)] = rate[0:16, 0:128]
        return c1, d1, s1, fdx, fsx

    c0, d0, s0 = (load(0, 0), load(1, 0), load(2, 0))
    c1, d1, s1 = (load(0, 1), load(1, 1), load(2, 1))
    start = (c1, d1, s1, (d0 + d1) * (c1 - c0), (s0 + s1) * (c1 - c0))
    carry = lax.fori_loop(0, n + 1, first, start)
    keep = r1[n - 1]
    first(n + 1, carry)
    r1[n - 1] = keep

    def second(x, carry):
        l0, t0, d0, s0, f1, f2, acc = carry
        t = x + 1
        l1, t1 = (later[t + 1], tang[t + 1])
        d1, s1 = (load(1, t + 2), load(2, t + 2))
        dsx = d0 + d1
        fl = dsx * (l1 - l0)
        ft = dsx * (t1 - t0) + (s0 + s1) * (l1 - l0)
        dy = d0 + up(d0, 0)
        gly = up(l0, 0) - l0
        fly = dy * gly
        fty = dy * (up(t0, 0) - t0) + (s0 + up(s0, 0)) * gly
        dz = d0 + up(d0, 1)
        glz = up(l0, 1) - l0
        flz = dz * glz
        ftz = dz * (up(t0, 1) - t0) + (s0 + up(s0, 1)) * glz
        vel = load(5, t + 1)
        vl = vel * l0
        vt = vel * t0
        rate = 0.5 * face_sum(fl, f1, fly, flz) + (down(vl, 1) - vl)
        other = 0.5 * face_sum(ft, f2, fty, ftz) + (down(vt, 1) - vt)
        rate = rate[0:16, 0:128]
        a = a_out[t + 1, 0:16, 0:128]
        final = t0[0:16, 0:128] + a * (other[0:16, 0:128] - q_s[t] * rate)
        r2[x] = rate
        acc = jnp.where(x % 8 == 0, 0.0, acc) + final
        cs[x // 8] = acc
        return l1, t1, d1, s1, fl, ft, acc

    l0, t0 = (later[0], tang[0])
    l1, t1 = (later[1], tang[1])
    d0, s0, d1, s1 = (load(1, 1), load(2, 1), load(1, 2), load(2, 2))
    start = (
        l1,
        t1,
        d1,
        s1,
        (d0 + d1) * (l1 - l0),
        (d0 + d1) * (t1 - t0) + (s0 + s1) * (l1 - l0),
        jnp.zeros((16, 128), F32),
    )
    lax.fori_loop(0, n, second, start)

    lane8 = lanes((8, 128))
    row8 = rows((8, 128))
    expand = (
        lanes((16, 128)) // 8 == rows((16, 128))
    ).astype(F32)
    for yv in range(2):
        out = jnp.zeros((8, 128), F32)
        for X in range(n // 8):
            q = cs[X, 8 * yv : 8 * yv + 8, :]
            for k in (1, 2, 4):
                q = q + pltpu.roll(q, k, 0)
            for k in (1, 2, 4):
                q = q + jnp.where(lane8 & k == 0, pltpu.roll(q, 128 - k, 1), pltpu.roll(q, k, 1))
            out = jnp.where(row8 == X + 1, q, out)
        kind = cls[yv]
        weight = jnp.zeros(kind.shape, F32)
        for k in range(cw.shape[0]):
            weight = jnp.where(kind == k, cw[k], weight)
        weight = weight * mask[yv].astype(F32)
        wide = jnp.dot(weight, expand, precision=lax.Precision.HIGHEST, preferred_element_type=F32)
        v_out[yv] = out * wide * (1.0 / 512.0)


def merge_x(idx, own, r0, r1, out):
    even = idx[0] == 0
    row = rows((8, 128))
    for yv in range(2):
        lo = jnp.where(even, r1[yv], r0[yv])
        hi = jnp.where(even, r0[yv], r1[yv])
        value = jnp.where(row == 0, pltpu.roll(lo, 2, 0), own[yv])
        out[yv] = jnp.where(row == 7, pltpu.roll(hi, 6, 0), value)


def merge_y(idx, own, r0, r1, out):
    even = idx[1] == 0
    out[0] = jnp.where(even, r1[1], r0[1])
    out[1] = own[0]
    out[2] = own[1]
    out[3] = jnp.where(even, r0[0], r1[0])


def adjoint(idx, vox, rz0, rz1, p, h, a_in, later, r1, r2, gd, gc, src, sc, sf):
    n = r1.shape[0]
    zeven = idx[2] == 0
    lane = lanes((8, 128))
    row = rows((8, 128))
    for X in range(n // 8 + 2):
        for side in range(2):
            parts = []
            for yv in range(4):
                if side == 0:
                    value = vox[yv, X : X + 1, :]
                else:
                    one, two = (rz0[yv, X : X + 1, :], rz1[yv, X : X + 1, :])
                    hi = jnp.where(zeven, one, two)
                    lo = jnp.where(zeven, two, one)
                    value = jnp.where(lane[0:1] < 64, hi, lo)
                parts.append(jnp.broadcast_to(value, (8, 128)))
            at = slice(128 * side, 128 * side + 128)
            src[X, 0:8, at] = parts[1]
            src[X, 8:16, at] = parts[2]
            src[X, 16:24, at] = jnp.where(row < 4, parts[3], parts[0])

    def load(f, e):
        return jnp.concatenate([p[f, e], h[(0, 1, None, None, None, 2)[f], e]], axis=1)

    def scale(e, _):
        sc[e] = a_in[e] * src[(e + 6) // 8]
        return 0

    lax.fori_loop(0, n + 4, scale, 0)

    def third(t, carry):
        m0, d0, f0 = carry
        e = t + 1
        m1, d1 = (sc[e + 1], load(1, e + 1))
        fx = (d0 + d1) * (m1 - m0)
        fy = (d0 + up(d0, 0)) * (up(m0, 0) - m0)
        gz = up(m0, 1) - m0
        fz = (d0 + up(d0, 1)) * gz
        earlier = src[(e + 6) // 8] + 0.5 * face_sum(fx, f0, fy, fz) + load(5, e) * gz
        sf[t] = a_in[e] * earlier
        return m1, d1, fx

    m0, m1, d0, d1 = (sc[0], sc[1], load(1, 0), load(1, 1))
    lax.fori_loop(0, n + 2, third, (m1, d1, (d0 + d1) * (m1 - m0)))

    def fourth(x, carry):
        m0, l0, s0, c0, e0 = carry
        t = x + 1
        m1, l1, s1, c1 = (sc[t + 2], later[t + 1], sf[t + 1], load(0, t + 2))
        ex = (m0 - m1) * (l1 - l0) + (s0 - s1) * (c1 - c0)
        ey = (m0 - up(m0, 0)) * (up(l0, 0) - l0) + (s0 - up(s0, 0)) * (up(c0, 0) - c0)
        ez = (m0 - up(m0, 1)) * (up(l0, 1) - l0) + (s0 - up(s0, 1)) * (up(c0, 1) - c0)
        total = (ex + e0) + (ey + down(ey, 0)) + (ez + down(ez, 1))
        gd[x] = 0.5 * total[0:16, 0:128]
        a = a_in[t + 1, 0:16, 0:128]
        gc[x] = (-1 / DT) * a * (m0[0:16, 0:128] * r2[x] + s0[0:16, 0:128] * r1[x])
        return m1, l1, s1, c1, ex

    m0, l0, s0, c0 = (sc[1], later[0], sf[0], load(0, 1))
    m1, l1, s1, c1 = (sc[2], later[1], sf[1], load(0, 2))
    lax.fori_loop(0, n, fourth, (m1, l1, s1, c1, (m0 - m1) * (l1 - l0) + (s0 - s1) * (c1 - c0)))


def coarse(x):
    x = jnp.transpose(x, (1, 0, 2))
    return jnp.pad(x, ((0, 0), (1, 1), (0, 0)))


def shards(c, d, s, cap, m, v, mask, cls, cw):
    n = c.shape[0]
    idx = jnp.stack([lax.axis_index(a) % 2 for a in ("gx", "gy", "gz")]).astype(jnp.int32)
    fields = (c, d, s, cap, m, v)
    bx = call(
        pack_x,
        [(10, 16, 128)] * 2,
        [SM] + [HB] * 6,
        (idx,) + fields,
        [pltpu.SemaphoreType.DMA((20,))],
    )
    rx = [swap(b, "gx", i) for i, b in enumerate(bx)]
    by = call(
        pack_y, [(n + 2 + n // 4, 8, 128)] * 2, [SM] + [VM] * 8, (idx,) + fields + tuple(rx)
    )
    ry = [swap(b, "gy", i) for i, b in enumerate(by)]
    p, t = call(
        pack_z,
        [(6, n + 4, 24, 128), ((n + 2) // 5, 24, 128)],
        [SM] + [VM] * 10,
        (idx,) + fields + tuple(rx) + tuple(ry),
    )
    rz = [swap(t, "gz", i) for i in range(2)]
    vox, h, a, later, r1, r2 = call(
        forward,
        [
            (2, 8, 128),
            (3, n + 4, 24, 128),
            (n + 4, 24, 256),
            (n + 2, 24, 256),
            (n, 16, 128),
            (n, 16, 128),
        ],
        [SM, SM] + [VM] * 5,
        (idx, cw, p, *rz, coarse(mask), coarse(cls)),
        [
            pltpu.VMEM((n + 2, 24, 256), F32),
            pltpu.VMEM((n + 2, 16, 128), F32),
            pltpu.VMEM((3, n + 4, 24, 128), F32),
            pltpu.VMEM((n // 8, 16, 128), F32),
        ],
    )
    rv = [swap(vox, "gx", i) for i in range(2)]
    (vox,) = call(merge_x, [(2, 8, 128)], [SM] + [VM] * 3, (idx, vox, *rv), limit=1)
    rv = [swap(vox, "gy", i) for i in range(2)]
    (vox,) = call(merge_y, [(4, 8, 128)], [SM] + [VM] * 3, (idx, vox, *rv), limit=1)
    rv = [swap(vox, "gz", i) for i in range(2)]
    gd, gc = call(
        adjoint,
        [(n, 16, 128)] * 2,
        [SM] + [VM] * 9,
        (idx, vox, *rv, p, h, a, later, r1, r2),
        [
            pltpu.VMEM((n // 8 + 2, 24, 256), F32),
            pltpu.VMEM((n + 4, 24, 256), F32),
            pltpu.VMEM((n + 2, 24, 256), F32),
        ],
    )
    return gd, gc


def solution(mesh):
    spec = P("gx", "gy", "gz")
    return jax.shard_map(
        shards, mesh=mesh, in_specs=(spec,) * 8 + (P(),), out_specs=(spec, spec), check_vma=False
    )
```

```python
import jax
import jax.numpy as jnp
from jax import lax
from jax.experimental import pallas as pl
from jax.experimental.pallas import tpu as pltpu
from jax.sharding import PartitionSpec as P

DT = 0.1
F32 = jnp.float32
VM = pl.BlockSpec(memory_space=pltpu.VMEM)
SM = pl.BlockSpec(memory_space=pltpu.SMEM)
HB = pl.BlockSpec(memory_space=pltpu.HBM)


def swap_pairs(size, first):
    pairs = []
    for i in range(first, size - 1, 2):
        pairs += [(i, i + 1), (i + 1, i)]
    return pairs


def swap(value, axis, first):
    return lax.ppermute(value, axis, swap_pairs(lax.axis_size(axis), first))


def call(body, outs, specs, args, scratch=(), limit=24, alias=None):
    return pl.pallas_call(
        body,
        out_shape=[jax.ShapeDtypeStruct(s, F32) for s in outs],
        in_specs=specs,
        out_specs=[VM] * len(outs),
        scratch_shapes=list(scratch),
        input_output_aliases=alias or {},
        compiler_params=pltpu.CompilerParams(vmem_limit_bytes=limit << 20),
    )(*args)


def rows(shape):
    return lax.broadcasted_iota(jnp.int32, shape, len(shape) - 2)


def lanes(shape):
    return lax.broadcasted_iota(jnp.int32, shape, len(shape) - 1)


def up(x, axis):
    return pltpu.roll(x, x.shape[axis] - 1, axis)


def down(x, axis):
    return pltpu.roll(x, 1, axis)


def rolled(x, shift, axis):
    shift = shift % x.shape[axis]
    return x if shift == 0 else pltpu.roll(x, shift, axis)


def pack_a(idx, c, d, s, cap, m, v, all_f, bx0, bx1, by0, by1, sems):
    n = c.shape[0]
    xeven = idx[0] == 0
    yeven = idx[1] == 0
    row = rows((8, 128))
    copies = [
        pltpu.make_async_copy(ref, all_f.at[f], sems.at[f])
        for f, ref in enumerate((c, d, s, cap, m, v))
    ]
    for copy in copies:
        copy.start()
    for copy in copies:
        copy.wait()
    for out, hi in ((bx0, xeven), (bx1, jnp.logical_not(xeven))):
        one = jnp.where(hi, n - 1, 0)
        two = jnp.where(hi, n - 2, 1)
        for slot, (f, at) in enumerate(
            [(f, i) for f in range(4) for i in (one, two)] + [(4, one), (5, one)]
        ):
            out[slot] = all_f[f, at]

    def tiles(four, low):
        out = None
        for f, value in enumerate(four):
            part = rolled(value, 2 * f if low else 2 * f + 2, 0)
            out = part if f == 0 else jnp.where(row < 2 * f, out, part)
        return out

    def put(at, lo, hi):
        by0[at] = jnp.where(yeven, hi, lo)
        by1[at] = jnp.where(yeven, lo, hi)

    def group(g, _):
        lo = hi = None
        for k in range(8):
            x = g * 4 + k // 2
            if k % 2 == 0:
                put(
                    x,
                    tiles([all_f[f, x, 0:8, :] for f in range(4)], True),
                    tiles([all_f[f, x, 8:16, :] for f in range(4)], False),
                )
            a = rolled(all_f[4 + k % 2, x, 0:8, :], k, 0)
            b = rolled(all_f[4 + k % 2, x, 8:16, :], k + 1, 0)
            lo = a if k == 0 else jnp.where(row < k, lo, a)
            hi = b if k == 0 else jnp.where(row < k, hi, b)
        put(n + g, lo, hi)
        return 0

    lax.fori_loop(0, n // 4, group, 0)


def pack_b(idx, all_f, rx0, rx1, ry0, ry1, p, t, e0, e1):
    n = all_f.shape[1]
    xeven = idx[0] == 0
    yeven = idx[1] == 0
    row = rows((8, 128))
    zero = jnp.zeros((8, 128), F32)

    def both(at):
        one, two = (ry0[at], ry1[at])
        return jnp.where(yeven, one, two), jnp.where(yeven, two, one)

    def group(g, _):
        mvhi, mvlo = both(n + g)
        for k in range(4):
            x = g * 4 + k
            hi, lo = both(x)
            for f in range(6):
                p[f, x + 2, 0:16, :] = all_f[f, x]
                if f < 4:
                    a, b = (rolled(hi, -2 * f, 0), rolled(lo, 6 - 2 * f, 0))
                else:
                    r = 2 * k + f - 4
                    a, b = (rolled(mvhi, -r, 0), rolled(mvlo, 7 - r, 0))
                p[f, x + 2, 16:24, :] = jnp.where(row < 4, a, b)
        return 0

    lax.fori_loop(0, n // 4, group, 0)
    for near, far, pick in ((1, 0, xeven), (n + 2, n + 3, jnp.logical_not(xeven))):
        for f in range(6):
            slot = 2 * f if f < 4 else 4 + f
            p[f, near, 0:16, :] = jnp.where(pick, rx1[slot], rx0[slot])
            p[f, far, 0:16, :] = (
                jnp.where(pick, rx1[slot + 1], rx0[slot + 1]) if f < 4 else jnp.zeros((16, 128), F32)
            )
            p[f, near, 16:24, :] = zero
            p[f, far, 16:24, :] = zero
    for f in range(4):
        lo, hi = (p[f, 2, 16:24, :], p[f, n + 1, 16:24, :])
        e0[f] = jnp.where(xeven, hi, lo)
        e1[f] = jnp.where(xeven, lo, hi)
    lane = lanes((24, 128))

    def pack(g, _):
        out = None
        for k in range(30):
            part = rolled(p[k % 6, g * 5 + k // 6 + 1], 4 * k + 2, 1)
            out = part if k == 0 else jnp.where(lane < 4 * k, out, part)
        t[g] = out
        return 0

    lax.fori_loop(0, (n + 2) // 5, pack, 0)


def face_sum(flux_x, flux_xm, flux_y, flux_z):
    return (flux_x - flux_xm) + (flux_y - down(flux_y, 0)) + (flux_z - down(flux_z, 1))


def forward(
    idx, cw, p_in, rz0, rz1, re0, re1, mask, cls, p, v_out, h, a_out, later, r1, r2, tang, q_s, hs, cs
):
    n = r1.shape[0]
    xeven = idx[0] == 0
    zeven = idx[2] == 0
    for f in range(4):
        p[f, 1, 16:24, :] = jnp.where(xeven, re1[f], re0[f])
        p[f, n + 2, 16:24, :] = jnp.where(xeven, re0[f], re1[f])
    lane = lanes((24, 128))

    def unpack(g, _):
        one, two = (rz0[g], rz1[g])
        hi = jnp.where(zeven, one, two)
        lo = jnp.where(zeven, two, one)
        both = jnp.where(lane % 4 < 2, lo, hi)
        for k in range(30):
            part = rolled(both, -(4 * k + 2), 1)
            f, e = (k % 6, g * 5 + k // 6 + 1)
            if f in (0, 1, 5):
                h[(0, 1, None, None, None, 2)[f], e] = part
            else:
                hs[f - 2, e] = part
        return 0

    lax.fori_loop(0, (n + 2) // 5, unpack, 0)
    for e in (0, n + 3):
        for k in range(3):
            h[k, e] = jnp.zeros((24, 128), F32)
            hs[k, e] = jnp.zeros((24, 128), F32)

    def load(f, e):
        halo = h[(0, 1, None, None, None, 2)[f], e] if f in (0, 1, 5) else hs[f - 2, e]
        return jnp.concatenate([p[f, e], halo], axis=1)

    def inverse(e):
        cap = load(3, e)
        a_out[e] = DT * jnp.where(cap > 0, 1.0 / jnp.where(cap > 0, cap, 1.0), 0.0)

    def make(e, _):
        inverse(e)
        return 0

    lax.fori_loop(0, n + 4, make, 0)

    def first(t, carry):
        c0, d0, s0, fd, fs = carry
        e = t + 1
        c1, d1, s1 = (load(0, e + 1), load(1, e + 1), load(2, e + 1))
        gx = c1 - c0
        fdx = (d0 + d1) * gx
        fsx = (s0 + s1) * gx
        gy = up(c0, 0) - c0
        fdy = (d0 + up(d0, 0)) * gy
        fsy = (s0 + up(s0, 0)) * gy
        gz = up(c0, 1) - c0
        fdz = (d0 + up(d0, 1)) * gz
        fsz = (s0 + up(s0, 1)) * gz
        vc = load(5, e) * c0
        rate = 0.5 * face_sum(fdx, fd, fdy, fdz) + (down(vc, 1) - vc)
        a = a_out[e]
        q = (1 / DT) * a * load(4, e)
        later[t] = c0 + a * rate
        tang[t] = a * (0.5 * face_sum(fsx, fs, fsy, fsz) - q * rate)
        q_s[t] = q[0:16, 0:128]
        r1[jnp.clip(t - 1, 0, n - 1)] = rate[0:16, 0:128]
        return c1, d1, s1, fdx, fsx

    c0, d0, s0 = (load(0, 0), load(1, 0), load(2, 0))
    c1, d1, s1 = (load(0, 1), load(1, 1), load(2, 1))
    start = (c1, d1, s1, (d0 + d1) * (c1 - c0), (s0 + s1) * (c1 - c0))
    carry = lax.fori_loop(0, n + 1, first, start)
    keep = r1[n - 1]
    first(n + 1, carry)
    r1[n - 1] = keep

    def second(x, carry):
        l0, t0, d0, s0, f1, f2, acc = carry
        t = x + 1
        l1, t1 = (later[t + 1], tang[t + 1])
        d1, s1 = (load(1, t + 2), load(2, t + 2))
        dsx = d0 + d1
        fl = dsx * (l1 - l0)
        ft = dsx * (t1 - t0) + (s0 + s1) * (l1 - l0)
        dy = d0 + up(d0, 0)
        gly = up(l0, 0) - l0
        fly = dy * gly
        fty = dy * (up(t0, 0) - t0) + (s0 + up(s0, 0)) * gly
        dz = d0 + up(d0, 1)
        glz = up(l0, 1) - l0
        flz = dz * glz
        ftz = dz * (up(t0, 1) - t0) + (s0 + up(s0, 1)) * glz
        vel = load(5, t + 1)
        vl = vel * l0
        vt = vel * t0
        rate = 0.5 * face_sum(fl, f1, fly, flz) + (down(vl, 1) - vl)
        other = 0.5 * face_sum(ft, f2, fty, ftz) + (down(vt, 1) - vt)
        rate = rate[0:16, 0:128]
        a = a_out[t + 1, 0:16, 0:128]
        final = t0[0:16, 0:128] + a * (other[0:16, 0:128] - q_s[t] * rate)
        r2[x] = rate
        acc = jnp.where(x % 8 == 0, 0.0, acc) + final
        cs[x // 8] = acc
        return l1, t1, d1, s1, fl, ft, acc

    l0, t0 = (later[0], tang[0])
    l1, t1 = (later[1], tang[1])
    d0, s0, d1, s1 = (load(1, 1), load(2, 1), load(1, 2), load(2, 2))
    start = (
        l1,
        t1,
        d1,
        s1,
        (d0 + d1) * (l1 - l0),
        (d0 + d1) * (t1 - t0) + (s0 + s1) * (l1 - l0),
        jnp.zeros((16, 128), F32),
    )
    lax.fori_loop(0, n, second, start)

    lane8 = lanes((8, 128))
    row8 = rows((8, 128))
    expand = (
        lanes((16, 128)) // 8 == rows((16, 128))
    ).astype(F32)
    for yv in range(2):
        out = jnp.zeros((8, 128), F32)
        for X in range(n // 8):
            q = cs[X, 8 * yv : 8 * yv + 8, :]
            for k in (1, 2, 4):
                q = q + pltpu.roll(q, k, 0)
            for k in (1, 2, 4):
                q = q + jnp.where(lane8 & k == 0, pltpu.roll(q, 128 - k, 1), pltpu.roll(q, k, 1))
            out = jnp.where(row8 == X + 1, q, out)
        kind = cls[yv]
        weight = jnp.zeros(kind.shape, F32)
        for k in range(cw.shape[0]):
            weight = jnp.where(kind == k, cw[k], weight)
        weight = weight * mask[yv].astype(F32)
        wide = jnp.dot(weight, expand, precision=lax.Precision.HIGHEST, preferred_element_type=F32)
        v_out[yv] = out * wide * (1.0 / 512.0)


def merge(idx, own, rx0, rx1, ry0, ry1, out, edge):
    xeven = idx[0] == 0
    yeven = idx[1] == 0
    row = rows((8, 128))
    for yv in range(2):
        lo = jnp.where(xeven, rx1[yv], rx0[yv])
        hi = jnp.where(xeven, rx0[yv], rx1[yv])
        value = jnp.where(row == 0, pltpu.roll(lo, 2, 0), own[yv])
        out[yv + 1] = jnp.where(row == 7, pltpu.roll(hi, 6, 0), value)
    for k, value in ((0, jnp.where(yeven, ry1[1], ry0[1])), (1, jnp.where(yeven, ry0[0], ry1[0]))):
        out[3 * k] = value
        edge[k] = value


def adjoint(idx, vox, rz0, rz1, re0, re1, p, h, a_in, later, r1, r2, gd, gc, src, sc, sf):
    n = r1.shape[0]
    zeven = idx[2] == 0
    lane = lanes((8, 128))
    row = rows((8, 128))
    xeven = idx[0] == 0
    last = n // 8 + 1
    for X in range(last + 1):
        for side in range(2):
            parts = []
            for yv in range(4):
                if side == 0 and X in (0, last) and yv in (0, 3):
                    at, k = (last - 1 if X == 0 else 1, yv // 3)
                    one, two = (re0[k, at : at + 1, :], re1[k, at : at + 1, :])
                    value = jnp.where(xeven, two, one) if X == 0 else jnp.where(xeven, one, two)
                elif side == 0:
                    value = vox[yv, X : X + 1, :]
                else:
                    one, two = (rz0[yv, X : X + 1, :], rz1[yv, X : X + 1, :])
                    hi = jnp.where(zeven, one, two)
                    lo = jnp.where(zeven, two, one)
                    value = jnp.where(lane[0:1] < 64, hi, lo)
                parts.append(jnp.broadcast_to(value, (8, 128)))
            at = slice(128 * side, 128 * side + 128)
            src[X, 0:8, at] = parts[1]
            src[X, 8:16, at] = parts[2]
            src[X, 16:24, at] = jnp.where(row < 4, parts[3], parts[0])

    def load(f, e):
        return jnp.concatenate([p[f, e], h[(0, 1, None, None, None, 2)[f], e]], axis=1)

    def scale(e, _):
        sc[e] = a_in[e] * src[(e + 6) // 8]
        return 0

    lax.fori_loop(0, n + 4, scale, 0)

    def third(t, carry):
        m0, d0, f0 = carry
        e = t + 1
        m1, d1 = (sc[e + 1], load(1, e + 1))
        fx = (d0 + d1) * (m1 - m0)
        fy = (d0 + up(d0, 0)) * (up(m0, 0) - m0)
        gz = up(m0, 1) - m0
        fz = (d0 + up(d0, 1)) * gz
        earlier = src[(e + 6) // 8] + 0.5 * face_sum(fx, f0, fy, fz) + load(5, e) * gz
        sf[t] = a_in[e] * earlier
        return m1, d1, fx

    m0, m1, d0, d1 = (sc[0], sc[1], load(1, 0), load(1, 1))
    lax.fori_loop(0, n + 2, third, (m1, d1, (d0 + d1) * (m1 - m0)))

    def fourth(x, carry):
        m0, l0, s0, c0, e0 = carry
        t = x + 1
        m1, l1, s1, c1 = (sc[t + 2], later[t + 1], sf[t + 1], load(0, t + 2))
        ex = (m0 - m1) * (l1 - l0) + (s0 - s1) * (c1 - c0)
        ey = (m0 - up(m0, 0)) * (up(l0, 0) - l0) + (s0 - up(s0, 0)) * (up(c0, 0) - c0)
        ez = (m0 - up(m0, 1)) * (up(l0, 1) - l0) + (s0 - up(s0, 1)) * (up(c0, 1) - c0)
        total = (ex + e0) + (ey + down(ey, 0)) + (ez + down(ez, 1))
        gd[x] = 0.5 * total[0:16, 0:128]
        a = a_in[t + 1, 0:16, 0:128]
        gc[x] = (-1 / DT) * a * (m0[0:16, 0:128] * r2[x] + s0[0:16, 0:128] * r1[x])
        return m1, l1, s1, c1, ex

    m0, l0, s0, c0 = (sc[1], later[0], sf[0], load(0, 1))
    m1, l1, s1, c1 = (sc[2], later[1], sf[1], load(0, 2))
    lax.fori_loop(0, n, fourth, (m1, l1, s1, c1, (m0 - m1) * (l1 - l0) + (s0 - s1) * (c1 - c0)))


def coarse(x):
    x = jnp.transpose(x, (1, 0, 2))
    return jnp.pad(x, ((0, 0), (1, 1), (0, 0)))


def shards(c, d, s, cap, m, v, mask, cls, cw):
    n = c.shape[0]
    idx = jnp.stack([lax.axis_index(a) % 2 for a in ("gx", "gy", "gz")]).astype(jnp.int32)
    fields = [pltpu.with_memory_space_constraint(f, pltpu.HBM) for f in (c, d, s, cap, m, v)]
    all_f, bx0, bx1, by0, by1 = call(
        pack_a,
        [(6, n, 16, 128)] + [(10, 16, 128)] * 2 + [(n + n // 4, 8, 128)] * 2,
        [SM] + [HB] * 6,
        (idx, *fields),
        [pltpu.SemaphoreType.DMA((6,))],
    )
    ry1 = swap(by1, "gy", 1)
    ry0 = swap(by0, "gy", 0)
    rx0 = swap(bx0, "gx", 0)
    rx1 = swap(bx1, "gx", 1)
    p, t, e0, e1 = call(
        pack_b,
        [(6, n + 4, 24, 128), ((n + 2) // 5, 24, 128), (4, 8, 128), (4, 8, 128)],
        [SM] + [VM] * 5,
        (idx, all_f, rx0, rx1, ry0, ry1),
    )
    rz1 = swap(t, "gz", 1)
    rz0 = swap(t, "gz", 0)
    re0 = swap(e0, "gx", 0)
    re1 = swap(e1, "gx", 1)
    p, vox, h, a, later, r1, r2 = call(
        forward,
        [
            (6, n + 4, 24, 128),
            (2, 8, 128),
            (3, n + 4, 24, 128),
            (n + 4, 24, 256),
            (n + 2, 24, 256),
            (n, 16, 128),
            (n, 16, 128),
        ],
        [SM, SM] + [VM] * 7,
        (idx, cw, p, rz0, rz1, re0, re1, coarse(mask), coarse(cls)),
        [
            pltpu.VMEM((n + 2, 24, 256), F32),
            pltpu.VMEM((n + 2, 16, 128), F32),
            pltpu.VMEM((3, n + 4, 24, 128), F32),
            pltpu.VMEM((n // 8, 16, 128), F32),
        ],
        alias={2: 0},
    )
    ry1 = swap(vox, "gy", 1)
    ry0 = swap(vox, "gy", 0)
    rx0 = swap(vox, "gx", 0)
    rx1 = swap(vox, "gx", 1)
    vox, edge = call(
        merge, [(4, 8, 128), (2, 8, 128)], [SM] + [VM] * 5, (idx, vox, rx0, rx1, ry0, ry1), limit=1
    )
    rz1 = swap(vox, "gz", 1)
    rz0 = swap(vox, "gz", 0)
    re0 = swap(edge, "gx", 0)
    re1 = swap(edge, "gx", 1)
    gd, gc = call(
        adjoint,
        [(n, 16, 128)] * 2,
        [SM] + [VM] * 11,
        (idx, vox, rz0, rz1, re0, re1, p, h, a, later, r1, r2),
        [
            pltpu.VMEM((n // 8 + 2, 24, 256), F32),
            pltpu.VMEM((n + 4, 24, 256), F32),
            pltpu.VMEM((n + 2, 24, 256), F32),
        ],
    )
    return gd, gc


def solution(mesh):
    spec = P("gx", "gy", "gz")
    return jax.shard_map(
        shards, mesh=mesh, in_specs=(spec,) * 8 + (P(),), out_specs=(spec, spec), check_vma=False
    )
```

```python
from functools import partial

import jax
import jax.numpy as jnp
from jax import lax
from jax.experimental import pallas as pl
from jax.experimental.pallas import tpu as pltpu
from jax.sharding import PartitionSpec as P

DT = 0.1
U1, U2, U3, U4 = (5, 4, 10, 8)
F32 = jnp.float32
VM = pl.BlockSpec(memory_space=pltpu.VMEM)
SM = pl.BlockSpec(memory_space=pltpu.SMEM)
HB = pl.BlockSpec(memory_space=pltpu.HBM)


def swap_pairs(size, first):
    pairs = []
    for i in range(first, size, 2):
        pairs += [(i, (i + 1) % size), ((i + 1) % size, i)]
    return pairs


def swap(value, axis, first):
    return lax.ppermute(value, axis, swap_pairs(lax.axis_size(axis), first))


def call(body, outs, specs, args, scratch=(), limit=24, alias=None):
    return pl.pallas_call(
        body,
        out_shape=[jax.ShapeDtypeStruct(s, F32) for s in outs],
        in_specs=specs,
        out_specs=[VM] * len(outs),
        scratch_shapes=list(scratch),
        input_output_aliases=alias or {},
        compiler_params=pltpu.CompilerParams(vmem_limit_bytes=limit << 20),
    )(*args)


def rows(shape):
    return lax.broadcasted_iota(jnp.int32, shape, len(shape) - 2)


def lanes(shape):
    return lax.broadcasted_iota(jnp.int32, shape, len(shape) - 1)


def up(x, axis):
    return pltpu.roll(x, x.shape[axis] - 1, axis)


def down(x, axis):
    return pltpu.roll(x, 1, axis)


def rolled(x, shift, axis):
    shift = shift % x.shape[axis]
    return x if shift == 0 else pltpu.roll(x, shift, axis)


def is_even(idx, axis):
    return idx[axis] % 2 == 0


def picked(ends, idx, axis, r0, r1):
    even = is_even(idx, axis)
    lo = jnp.where(even, r1, r0)
    hi = jnp.where(even, r0, r1)
    return jnp.where(idx[axis] > 0, lo, 0.0), jnp.where(idx[axis] < ends[axis], hi, 0.0)


def pack_a(idx, c, d, s, cap, m, v, all_f, bx0, bx1, by0, by1, sems):
    n = c.shape[0]
    xeven = is_even(idx, 0)
    yeven = is_even(idx, 1)
    row = rows((8, 128))
    copies = [
        pltpu.make_async_copy(ref, all_f.at[f], sems.at[f])
        for f, ref in enumerate((c, d, s, cap, m, v))
    ]
    for copy in copies:
        copy.start()
    for copy in copies:
        copy.wait()
    for out, hi in ((bx0, xeven), (bx1, jnp.logical_not(xeven))):
        one = jnp.where(hi, n - 1, 0)
        two = jnp.where(hi, n - 2, 1)
        for slot, (f, at) in enumerate(
            [(f, i) for f in range(4) for i in (one, two)] + [(4, one), (5, one)]
        ):
            out[slot] = all_f[f, at]

    def tiles(four, low):
        out = None
        for f, value in enumerate(four):
            part = rolled(value, 2 * f if low else 2 * f + 2, 0)
            out = part if f == 0 else jnp.where(row < 2 * f, out, part)
        return out

    def put(at, lo, hi):
        by0[at] = jnp.where(yeven, hi, lo)
        by1[at] = jnp.where(yeven, lo, hi)

    def group(g, _):
        lo = hi = None
        for k in range(8):
            x = g * 4 + k // 2
            if k % 2 == 0:
                put(
                    x,
                    tiles([all_f[f, x, 0:8, :] for f in range(4)], True),
                    tiles([all_f[f, x, 8:16, :] for f in range(4)], False),
                )
            a = rolled(all_f[4 + k % 2, x, 0:8, :], k, 0)
            b = rolled(all_f[4 + k % 2, x, 8:16, :], k + 1, 0)
            lo = a if k == 0 else jnp.where(row < k, lo, a)
            hi = b if k == 0 else jnp.where(row < k, hi, b)
        put(n + g, lo, hi)
        return 0

    lax.fori_loop(0, n // 4, group, 0)


def pack_b(ends, idx, all_f, rx0, rx1, ry0, ry1, p, t, e0, e1):
    n = all_f.shape[1]
    xeven = is_even(idx, 0)
    yeven = is_even(idx, 1)
    row = rows((8, 128))
    zero = jnp.zeros((8, 128), F32)

    def both(at):
        return picked(ends, idx, 1, ry0[at], ry1[at])

    def group(g, _):
        mvlo, mvhi = both(n + g)
        for k in range(4):
            x = g * 4 + k
            lo, hi = both(x)
            for f in range(6):
                p[f, x + 2, 0:16, :] = all_f[f, x]
                if f < 4:
                    a, b = (rolled(hi, -2 * f, 0), rolled(lo, 6 - 2 * f, 0))
                else:
                    r = 2 * k + f - 4
                    a, b = (rolled(mvhi, -r, 0), rolled(mvlo, 7 - r, 0))
                p[f, x + 2, 16:24, :] = jnp.where(row < 4, a, b)
        return 0

    lax.fori_loop(0, n // 4, group, 0)
    for f in range(6):
        slot = 2 * f if f < 4 else 4 + f
        p[f, 1, 0:16, :], p[f, n + 2, 0:16, :] = picked(ends, idx, 0, rx0[slot], rx1[slot])
        if f < 4:
            p[f, 0, 0:16, :], p[f, n + 3, 0:16, :] = picked(ends, idx, 0, rx0[slot + 1], rx1[slot + 1])
        else:
            p[f, 0, 0:16, :] = jnp.zeros((16, 128), F32)
            p[f, n + 3, 0:16, :] = jnp.zeros((16, 128), F32)
        for e in (0, 1, n + 2, n + 3):
            p[f, e, 16:24, :] = zero
    for f in range(4):
        lo, hi = (p[f, 2, 16:24, :], p[f, n + 1, 16:24, :])
        e0[f] = jnp.where(xeven, hi, lo)
        e1[f] = jnp.where(xeven, lo, hi)
    for f in range(6):
        for e in range(n + 4, p.shape[1]):
            p[f, e] = jnp.zeros((24, 128), F32)
    lane = lanes((24, 128))
    t[...] = jnp.zeros(t.shape, F32)

    def pack(g, _):
        for f in range(6):
            out = None
            for k in range(8):
                part = rolled(p[f, g * 8 + k], 4 * k + 2, 1)
                out = part if k == 0 else jnp.where(lane < 4 * k, out, part)
            out = pltpu.roll(out, (g & 3) * 32, 1)
            t[f, g >> 2] = jnp.where(lane // 32 == (g & 3), out, t[f, g >> 2])
        return 0

    lax.fori_loop(0, p.shape[1] // 8, pack, 0)


def wide(ref):
    return jnp.concatenate([ref[0], ref[1]], axis=1)


def ends_up(own, halo, slot):
    return jnp.where(slot == 1, up(own, 1), up(halo, 1))


def ends_down(own, halo, slot):
    return jnp.where(slot == 2, down(own, 1), down(halo, 1))


def ends_flow(k, f):
    kc, ku, kd = k
    fc, fu, fd = f
    fx = (kc + rolled(kc, -4, 1)) * (rolled(fc, -4, 1) - fc)
    fy = (kc + up(kc, 0)) * (up(fc, 0) - fc)
    flux = (fx - rolled(fx, 4, 1)) + (fy - down(fy, 0))
    return flux + ((kc + ku) * (fu - fc) - (kc + kd) * (fc - fd))


def to_ends(store, at, value, slot):
    value = jnp.where(slot == 1, up(value, 1), down(value, 1))
    store[at, 0] = value[:, 0:128]
    store[at, 1] = value[:, 128:256]


def edge(store, at, e, height=24):
    return pltpu.roll(store[at, e >> 5, 0:height, :], (126 - 4 * (e & 31)) & 127, 1)


def zflux(k0, f0, kh, fh, lane):
    ku = jnp.where(lane == 127, kh, up(k0, 1))
    fu = jnp.where(lane == 127, fh, up(f0, 1))
    return (k0 + ku) * (fu - f0)


def back(value, first, lane):
    return jnp.where(lane == 0, first, down(value, 1))


def inverse(cap):
    return DT * jnp.where(cap > 0, 1.0 / jnp.where(cap > 0, cap, 1.0), 0.0)


def forward(
    ends, idx, cw, p_in, t, rz0, rz1, re0, re1, mask, cls,
    p, v_out, h, a_out, later, later_z, r1, r2, tang, q_s, m, cs,
):
    n = r2.shape[0]
    for f in range(4):
        p[f, 1, 16:24, :], p[f, n + 2, 16:24, :] = picked(ends, idx, 0, re0[f], re1[f])

    slot = lanes((24, 256)) % 4
    own, halo = ([], [])
    for f in range(6):
        for col in range(2):
            lo, hi = picked(ends, idx, 2, rz0[f, col], rz1[f, col])
            h[f, col] = jnp.where(slot[:, 0:128] < 2, lo, hi)
        own.append(wide(t.at[f]))
        halo.append(wide(h.at[f]))
    near = [
        (halo[f], ends_up(own[f], halo[f], slot), ends_down(own[f], halo[f], slot)) for f in (0, 1, 2)
    ]
    vel, vel_down = (halo[5], ends_down(own[5], halo[5], slot))
    az = inverse(halo[3])
    qz = (1 / DT) * az * halo[4]
    rate = 0.5 * ends_flow(near[1], near[0]) + (vel_down * near[0][2] - vel * near[0][0])
    lz = near[0][0] + az * rate
    tz = az * (0.5 * ends_flow(near[2], near[0]) - qz * rate)
    later_z[0] = lz[:, 0:128]
    later_z[1] = lz[:, 128:256]
    for at, value in enumerate((halo[0], halo[1], halo[2], halo[5], lz, tz)):
        to_ends(m, at, value, slot)

    def make(e, _):
        a_out[e] = inverse(p[3, e])
        return 0

    lax.fori_loop(0, n + 4, make, 0, unroll=4)
    lane = lanes((24, 128))

    def first(t, carry):
        c0, d0, s0, fd, fs = carry
        e = t + 1
        c1, d1, s1 = (p[0, e + 1], p[1, e + 1], p[2, e + 1])
        ch, dh, sh, vh = (edge(m, k, e) for k in range(4))
        gx = c1 - c0
        fdx = (d0 + d1) * gx
        fsx = (s0 + s1) * gx
        gy = up(c0, 0) - c0
        fdy = (d0 + up(d0, 0)) * gy
        fsy = (s0 + up(s0, 0)) * gy
        gz = jnp.where(lane == 127, ch, up(c0, 1)) - c0
        fdz = (d0 + jnp.where(lane == 127, dh, up(d0, 1))) * gz
        fsz = (s0 + jnp.where(lane == 127, sh, up(s0, 1))) * gz
        gl = c0 - ch
        vc = p[5, e] * c0
        rate = (fdx - fd) + (fdy - down(fdy, 0)) + (fdz - back(fdz, (d0 + dh) * gl, lane))
        rate = 0.5 * rate + (back(vc, vh * ch, lane) - vc)
        other = (fsx - fs) + (fsy - down(fsy, 0)) + (fsz - back(fsz, (s0 + sh) * gl, lane))
        a = a_out[e]
        q = (1 / DT) * a * p[4, e]
        later[t] = c0 + a * rate
        tang[t] = a * (0.5 * other - q * rate)
        q_s[t] = q[0:16]
        r1[t] = rate[0:16]
        return c1, d1, s1, fdx, fsx

    c0, d0, s0 = (p[0, 0], p[1, 0], p[2, 0])
    c1, d1, s1 = (p[0, 1], p[1, 1], p[2, 1])
    start = (c1, d1, s1, (d0 + d1) * (c1 - c0), (s0 + s1) * (c1 - c0))
    lax.fori_loop(0, n + 2, first, start, unroll=U1)
    lane = lane[0:16]

    def second(x, carry):
        f1, f2, acc = carry
        t = x + 1
        e = t + 1
        l3, t3, d3, s3 = (later[t], tang[t], p[1, e], p[2, e])
        l0, t0, d0, s0 = (q[0:16] for q in (l3, t3, d3, s3))
        gl = later[t + 1, 0:16, :] - l0
        gt = tang[t + 1, 0:16, :] - t0
        dd = d0 + p[1, e + 1, 0:16, :]
        ss = s0 + p[2, e + 1, 0:16, :]
        fl = dd * gl
        ft = dd * gt + ss * gl
        dd = d3 + up(d3, 0)
        gly = up(l3, 0) - l3
        fly = dd * gly
        fty = dd * (up(t3, 0) - t3) + (s3 + up(s3, 0)) * gly
        dh, sh, vh, lh, th = (edge(m, k, e, 16) for k in (1, 2, 3, 4, 5))
        gl = jnp.where(lane == 127, lh, up(l0, 1)) - l0
        gt = jnp.where(lane == 127, th, up(t0, 1)) - t0
        dd = d0 + jnp.where(lane == 127, dh, up(d0, 1))
        ss = s0 + jnp.where(lane == 127, sh, up(s0, 1))
        flz = dd * gl
        ftz = dd * gt + ss * gl
        dd = d0 + dh
        gl = l0 - lh
        flb = back(flz, dd * gl, lane)
        ftb = back(ftz, dd * (t0 - th) + (s0 + sh) * gl, lane)
        vel = p[5, e, 0:16, :]
        vl = vel * l0
        vt = vel * t0
        rate = (fl - f1) + (fly - down(fly, 0))[0:16] + (flz - flb)
        rate = 0.5 * rate + (back(vl, vh * lh, lane) - vl)
        other = (ft - f2) + (fty - down(fty, 0))[0:16] + (ftz - ftb)
        other = 0.5 * other + (back(vt, vh * th, lane) - vt)
        final = t0 + a_out[e, 0:16, :] * (other - q_s[t] * rate)
        r2[x] = rate
        acc = jnp.where(x & 7 == 0, 0.0, acc) + final
        cs[x >> 3] = acc
        return fl, ft, acc

    gl = later[1, 0:16, :] - later[0, 0:16, :]
    gt = tang[1, 0:16, :] - tang[0, 0:16, :]
    dd = p[1, 1, 0:16, :] + p[1, 2, 0:16, :]
    ss = p[2, 1, 0:16, :] + p[2, 2, 0:16, :]
    lax.fori_loop(0, n, second, (dd * gl, dd * gt + ss * gl, jnp.zeros((16, 128), F32)), unroll=U2)

    lane8 = lanes((8, 128))
    row8 = rows((8, 128))
    expand = (
        lanes((16, 128)) // 8 == rows((16, 128))
    ).astype(F32)
    for yv in range(2):
        out = jnp.zeros((8, 128), F32)
        for X in range(n // 8):
            q = cs[X, 8 * yv : 8 * yv + 8, :]
            for k in (1, 2, 4):
                q = q + pltpu.roll(q, k, 0)
            for k in (1, 2, 4):
                q = q + jnp.where(lane8 & k == 0, pltpu.roll(q, 128 - k, 1), pltpu.roll(q, k, 1))
            out = jnp.where(row8 == X + 1, q, out)
        kind = cls[yv]
        weight = jnp.zeros(kind.shape, F32)
        for k in range(cw.shape[0]):
            weight = jnp.where(kind == k, cw[k], weight)
        weight = weight * mask[yv].astype(F32)
        spread = jnp.dot(weight, expand, precision=lax.Precision.HIGHEST, preferred_element_type=F32)
        v_out[yv] = out * spread * (1.0 / 512.0)


def merge(ends, idx, own, rx0, rx1, ry0, ry1, out, edge):
    xeven = is_even(idx, 0)
    yeven = is_even(idx, 1)
    row = rows((8, 128))
    for yv in range(2):
        lo, hi = picked(ends, idx, 0, rx0[yv], rx1[yv])
        value = jnp.where(row == 0, pltpu.roll(lo, 2, 0), own[yv])
        out[yv + 1] = jnp.where(row == 7, pltpu.roll(hi, 6, 0), value)
    lo = picked(ends, idx, 1, ry0[1], ry1[1])[0]
    hi = picked(ends, idx, 1, ry0[0], ry1[0])[1]
    for k, value in ((0, lo), (1, hi)):
        out[3 * k] = value
        edge[k] = value


def adjoint(
    ends, idx, vox, rz0, rz1, re0, re1, p, t, h, a_in, later, later_z, r1, r2,
    gd, gc, src, sc, sf, m,
):
    n = r2.shape[0]
    last = n // 8 + 1
    row = rows((8, 128))
    for X in range(last + 1):
        parts = []
        for yv in range(4):
            if X in (0, last) and yv in (0, 3):
                at, k = (last - 1 if X == 0 else 1, yv // 3)
                value = picked(ends, idx, 0, re0[k, at : at + 1, :], re1[k, at : at + 1, :])[X > 0]
            else:
                value = vox[yv, X : X + 1, :]
            parts.append(jnp.broadcast_to(value, (8, 128)))
        src[X, 0:8, :] = parts[1]
        src[X, 8:16, :] = parts[2]
        src[X, 16:24, :] = jnp.where(row < 4, parts[3], parts[0])

    slot8 = lanes((8, 128)) % 4
    sources = []
    for halo in (False, True):
        cols = []
        for col in range(2):
            here = (lanes((8, 128)) // 4 + 32 * col + 6) // 8 == row
            parts = []
            for yv in range(4):
                lo, hi = picked(ends, idx, 2, rz0[yv], rz1[yv]) if halo else (vox[yv], vox[yv])
                lo = jnp.broadcast_to(lo[:, 127:128], (8, 128))
                hi = jnp.broadcast_to(hi[:, 0:1], (8, 128))
                both = jnp.where(here, jnp.where(slot8 < 2, lo, hi), 0.0)
                for k in (1, 2, 4):
                    both = both + pltpu.roll(both, k, 0)
                parts.append(both)
            cols.append(
                jnp.concatenate([parts[1], parts[2], jnp.where(row < 4, parts[3], parts[0])], axis=0)
            )
        sources.append(jnp.concatenate(cols, axis=1))

    slot = lanes((24, 256)) % 4
    at, ah = (inverse(wide(t.at[3])), inverse(wide(h.at[3])))
    st, sh = (at * sources[0], ah * sources[1])
    dt, dh = (wide(t.at[1]), wide(h.at[1]))
    su = ends_up(st, sh, slot)
    flow = ends_flow(
        (dh, ends_up(dt, dh, slot), ends_down(dt, dh, slot)), (sh, su, ends_down(st, sh, slot))
    )
    fz = ah * (sources[1] + 0.5 * flow + wide(h.at[5]) * (su - sh))
    for k, value in enumerate((wide(h.at[0]), dh, sh, fz, wide(later_z))):
        to_ends(m, k, value, slot)

    def scale(e, _):
        sc[e] = a_in[e] * src[(e + 6) >> 3]
        return 0

    lax.fori_loop(0, n + 4, scale, 0, unroll=4)
    lane = lanes((24, 128))

    def third(t, f0):
        e = t + 1
        m0, d0 = (sc[e], p[1, e])
        dh, mh = (edge(m, 1, e), edge(m, 2, e))
        fx = (d0 + p[1, e + 1]) * (sc[e + 1] - m0)
        fy = (d0 + up(d0, 0)) * (up(m0, 0) - m0)
        gz = jnp.where(lane == 127, mh, up(m0, 1)) - m0
        fz = (d0 + jnp.where(lane == 127, dh, up(d0, 1))) * gz
        flow = (fx - f0) + (fy - down(fy, 0)) + (fz - back(fz, (d0 + dh) * (m0 - mh), lane))
        sf[t] = a_in[e] * (src[(e + 6) >> 3] + 0.5 * flow + p[5, e] * gz)
        return fx

    lax.fori_loop(0, n + 2, third, (p[1, 0] + p[1, 1]) * (sc[1] - sc[0]), unroll=U3)
    lane = lane[0:16]

    def fourth(x, e0):
        t = x + 1
        e = t + 1
        full = (sc[e], later[t], sf[t], p[0, e])
        m0, l0, s0, c0 = (q[0:16] for q in full)
        ex = (m0 - sc[e + 1, 0:16, :]) * (later[t + 1, 0:16, :] - l0)
        ex = ex + (s0 - sf[t + 1, 0:16, :]) * (p[0, e + 1, 0:16, :] - c0)
        m3, l3, s3, c3 = full
        ey = (m3 - up(m3, 0)) * (up(l3, 0) - l3) + (s3 - up(s3, 0)) * (up(c3, 0) - c3)
        ch, mh, sh, lh = (edge(m, k, e, 16) for k in (0, 2, 3, 4))
        mu, lu, su, cu = (
            jnp.where(lane == 127, b, up(a, 1)) for a, b in ((m0, mh), (l0, lh), (s0, sh), (c0, ch))
        )
        ez = (m0 - mu) * (lu - l0) + (s0 - su) * (cu - c0)
        eb = back(ez, (mh - m0) * (l0 - lh) + (sh - s0) * (c0 - ch), lane)
        gd[x] = 0.5 * ((ex + e0) + (ey + down(ey, 0))[0:16] + (ez + eb))
        gc[x] = (-1 / DT) * a_in[e, 0:16, :] * (m0 * r2[x] + s0 * r1[t])
        return ex

    ex = (sc[1, 0:16, :] - sc[2, 0:16, :]) * (later[1, 0:16, :] - later[0, 0:16, :])
    ex = ex + (sf[0, 0:16, :] - sf[1, 0:16, :]) * (p[0, 2, 0:16, :] - p[0, 1, 0:16, :])
    lax.fori_loop(0, n, fourth, ex, unroll=U4)


def coarse(x):
    x = jnp.transpose(x, (1, 0, 2))
    return jnp.pad(x, ((0, 0), (1, 1), (0, 0)))


def shards(c, d, s, cap, m, v, mask, cls, cw):
    n = c.shape[0]
    ends = [lax.axis_size(a) - 1 for a in ("gx", "gy", "gz")]
    idx = jnp.stack([lax.axis_index(a) for a in ("gx", "gy", "gz")]).astype(jnp.int32)
    fields = [pltpu.with_memory_space_constraint(f, pltpu.HBM) for f in (c, d, s, cap, m, v)]
    all_f, bx0, bx1, by0, by1 = call(
        pack_a,
        [(6, n, 16, 128)] + [(10, 16, 128)] * 2 + [(n + n // 4, 8, 128)] * 2,
        [SM] + [HB] * 6,
        (idx, *fields),
        [pltpu.SemaphoreType.DMA((6,))],
    )
    ry1 = swap(by1, "gy", 1)
    ry0 = swap(by0, "gy", 0)
    rx0 = swap(bx0, "gx", 0)
    rx1 = swap(bx1, "gx", 1)
    p, t, e0, e1 = call(
        partial(pack_b, ends),
        [(6, n + 8, 24, 128), (6, 2, 24, 128), (4, 8, 128), (4, 8, 128)],
        [SM] + [VM] * 5,
        (idx, all_f, rx0, rx1, ry0, ry1),
    )
    rz1 = swap(t, "gz", 1)
    rz0 = swap(t, "gz", 0)
    re0 = swap(e0, "gx", 0)
    re1 = swap(e1, "gx", 1)
    p, vox, h, a, later, later_z, r1, r2 = call(
        partial(forward, ends),
        [
            (6, n + 8, 24, 128),
            (2, 8, 128),
            (6, 2, 24, 128),
            (n + 4, 24, 128),
            (n + 2, 24, 128),
            (2, 24, 128),
            (n + 2, 16, 128),
            (n, 16, 128),
        ],
        [SM, SM] + [VM] * 8,
        (idx, cw, p, t, rz0, rz1, re0, re1, coarse(mask), coarse(cls)),
        [
            pltpu.VMEM((n + 2, 24, 128), F32),
            pltpu.VMEM((n + 2, 16, 128), F32),
            pltpu.VMEM((6, 2, 24, 128), F32),
            pltpu.VMEM((n // 8, 16, 128), F32),
        ],
        alias={2: 0},
    )
    ry1 = swap(vox, "gy", 1)
    ry0 = swap(vox, "gy", 0)
    rx0 = swap(vox, "gx", 0)
    rx1 = swap(vox, "gx", 1)
    vox, edge = call(
        partial(merge, ends), [(4, 8, 128), (2, 8, 128)], [SM] + [VM] * 5, (idx, vox, rx0, rx1, ry0, ry1), limit=1
    )
    rz1 = swap(vox, "gz", 1)
    rz0 = swap(vox, "gz", 0)
    re0 = swap(edge, "gx", 0)
    re1 = swap(edge, "gx", 1)
    gd, gc = call(
        partial(adjoint, ends),
        [(n, 16, 128)] * 2,
        [SM] + [VM] * 13,
        (idx, vox, rz0, rz1, re0, re1, p, t, h, a, later, later_z, r1, r2),
        [
            pltpu.VMEM((n // 8 + 2, 24, 128), F32),
            pltpu.VMEM((n + 4, 24, 128), F32),
            pltpu.VMEM((n + 2, 24, 128), F32),
            pltpu.VMEM((5, 2, 24, 128), F32),
        ],
    )
    return gd, gc


def solution(mesh):
    spec = P("gx", "gy", "gz")
    return jax.shard_map(
        shards, mesh=mesh, in_specs=(spec,) * 8 + (P(),), out_specs=(spec, spec), check_vma=False
    )
```

```python
from functools import partial

import jax
import jax.numpy as jnp
from jax import lax
from jax.experimental import pallas as pl
from jax.experimental.pallas import tpu as pltpu
from jax.sharding import PartitionSpec as P


DT = 0.1
U1, U2, U3, U4 = (5, 4, 10, 8)
F32 = jnp.float32
VM = pl.BlockSpec(memory_space=pltpu.VMEM)
SM = pl.BlockSpec(memory_space=pltpu.SMEM)
HB = pl.BlockSpec(memory_space=pltpu.HBM)


def swap_pairs(size, first):
    pairs = []
    for i in range(first, size, 2):
        pairs += [(i, (i + 1) % size), ((i + 1) % size, i)]
    return pairs


def swap(value, axis, first):
    return lax.ppermute(value, axis, swap_pairs(lax.axis_size(axis), first))


def call(body, outs, specs, args, scratch=(), limit=24, alias=None):
    return pl.pallas_call(
        body,
        out_shape=[jax.ShapeDtypeStruct(s, F32) for s in outs],
        in_specs=specs,
        out_specs=[VM] * len(outs),
        scratch_shapes=list(scratch),
        input_output_aliases=alias or {},
        compiler_params=pltpu.CompilerParams(vmem_limit_bytes=limit << 20),
    )(*args)


def rows(shape):
    return lax.broadcasted_iota(jnp.int32, shape, len(shape) - 2)


def lanes(shape):
    return lax.broadcasted_iota(jnp.int32, shape, len(shape) - 1)


def up(x, axis):
    return pltpu.roll(x, x.shape[axis] - 1, axis)


def down(x, axis):
    return pltpu.roll(x, 1, axis)


def rolled(x, shift, axis):
    shift = shift % x.shape[axis]
    return x if shift == 0 else pltpu.roll(x, shift, axis)


def is_even(idx, axis):
    return idx[axis] % 2 == 0


def picked(ends, idx, axis, r0, r1):
    even = is_even(idx, axis)
    lo = jnp.where(even, r1, r0)
    hi = jnp.where(even, r0, r1)
    return jnp.where(idx[axis] > 0, lo, 0.0), jnp.where(idx[axis] < ends[axis], hi, 0.0)


def pack_a(idx, c, d, s, cap, m, v, all_f, bx0, bx1, by0, by1, ys0, ys1, sems):
    n = c.shape[0]
    xeven = is_even(idx, 0)
    yeven = is_even(idx, 1)
    row = rows((8, 128))
    copies = [
        pltpu.make_async_copy(ref, all_f.at[f], sems.at[f])
        for f, ref in enumerate((c, d, s, cap, m, v))
    ]
    for copy in copies:
        copy.start()
    for copy in copies:
        copy.wait()
    for out, hi in ((bx0, xeven), (bx1, jnp.logical_not(xeven))):
        one = jnp.where(hi, n - 1, 0)
        two = jnp.where(hi, n - 2, 1)
        for slot, (f, at) in enumerate(
            [(f, i) for f in range(4) for i in (one, two)] + [(4, one), (5, one)]
        ):
            out[slot] = all_f[f, at]

    def tiles(four, low):
        out = None
        for f, value in enumerate(four):
            part = rolled(value, 2 * f if low else 2 * f + 2, 0)
            out = part if f == 0 else jnp.where(row < 2 * f, out, part)
        return out

    def put(at, lo, hi):
        by0[at] = jnp.where(yeven, hi, lo)
        by1[at] = jnp.where(yeven, lo, hi)

    def group(g, _):
        lo = hi = None
        for k in range(8):
            x = g * 4 + k // 2
            if k % 2 == 0:
                put(
                    x,
                    tiles([all_f[f, x, 0:8, :] for f in range(4)], True),
                    tiles([all_f[f, x, 8:16, :] for f in range(4)], False),
                )
            a = rolled(all_f[4 + k % 2, x, 0:8, :], k, 0)
            b = rolled(all_f[4 + k % 2, x, 8:16, :], k + 1, 0)
            lo = a if k == 0 else jnp.where(row < k, lo, a)
            hi = b if k == 0 else jnp.where(row < k, hi, b)
        put(n + g, lo, hi)
        return 0

    lax.fori_loop(0, n // 4, group, 0, unroll=2)
    lane = lanes((8, 128))
    for ys in (ys0, ys1):
        ys[0:4] = jnp.zeros((4, 8, 128), F32)
    for ys, by in ((ys0, by0), (ys1, by1)):
        ys[4] = by[0]
        ys[5] = by[n - 1]

    def ends_of(g, _):
        out = [None] * 4
        for k in range(8):
            x = g * 8 + k
            parts = (by0[x], by1[x], all_f[5, x, 0:8, :], all_f[5, x, 8:16, :])
            for i, value in enumerate(parts):
                part = rolled(value, 4 * k + 2, 1)
                out[i] = part if k == 0 else jnp.where(lane < 4 * k, out[i], part)
        at = g * 32 + 8
        for col in range(2):
            shift = (at - 128 * col) & 127
            here = (lane + 128 * col >= at) & (lane + 128 * col < at + 32)
            one, two, low, high = (pltpu.roll(q, shift, 1) for q in out)
            v0 = jnp.where(yeven, high, low)
            v1 = jnp.where(yeven, low, high)
            for ys, i, value in ((ys0, 0, one), (ys1, 0, two), (ys0, 2, v0), (ys1, 2, v1)):
                ys[i + col] = jnp.where(here, value, ys[i + col])
        return 0

    lax.fori_loop(0, n // 8, ends_of, 0, unroll=2)


def pack_t(all_f, t):
    n = all_f.shape[1]
    lane = lanes((16, 128))
    t[...] = jnp.zeros(t.shape, F32)

    def pack(g, _):
        at = g * 32 + 8
        for f in range(6):
            out = None
            for k in range(8):
                part = rolled(all_f[f, g * 8 + k], 4 * k + 2, 1)
                out = part if k == 0 else jnp.where(lane < 4 * k, out, part)
            out = pltpu.roll(out, at & 127, 1)
            for col in range(2):
                here = (lane + 128 * col >= at) & (lane + 128 * col < at + 32)
                t[f, col] = jnp.where(here, out, t[f, col])
        return 0

    lax.fori_loop(0, n // 8, pack, 0)


def third(hi, lo, f):
    row = rows((8, 128))
    return jnp.where(row < 4, rolled(hi, -2 * f, 0), rolled(lo, 6 - 2 * f, 0))


def pack_b(ends, planes, idx, tm, rx0, rx1, ys0, ys1, t, e0, e1):
    xeven = is_even(idx, 0)
    row = rows((8, 128))
    lane = lanes((16, 128))
    tiles = [picked(ends, idx, 1, ys0[k], ys1[k]) for k in range(6)]
    for f in range(6):
        halo = picked(ends, idx, 0, rx0[2 * f if f < 4 else 4 + f], rx1[2 * f if f < 4 else 4 + f])
        for col in range(2):
            at = (1, planes + 2)[col]
            part = rolled(halo[col], 4 * at + 2, 1)
            t[f, col, 0:16, :] = jnp.where(lane // 4 == at % 32, part, tm[f, col])
            if f < 4:
                t[f, col, 16:24, :] = third(tiles[col][1], tiles[col][0], f)
            elif f == 4:
                t[f, col, 16:24, :] = jnp.zeros((8, 128), F32)
            else:
                t[f, col, 16:24, :] = jnp.where(row < 4, tiles[2 + col][1], tiles[2 + col][0])
    for f in range(4):
        lo, hi = (third(tiles[k][1], tiles[k][0], f) for k in (4, 5))
        e0[f] = jnp.where(xeven, hi, lo)
        e1[f] = jnp.where(xeven, lo, hi)


def pack_c(ends, idx, all_f, rx0, rx1, ry0, ry1, p):
    n = all_f.shape[1]
    row = rows((8, 128))
    zero = jnp.zeros((8, 128), F32)

    def both(at):
        return picked(ends, idx, 1, ry0[at], ry1[at])

    def group(g, _):
        mvlo, mvhi = both(n + g)
        for k in range(4):
            x = g * 4 + k
            lo, hi = both(x)
            for f in range(6):
                p[f, x + 2, 0:16, :] = all_f[f, x]
                if f < 4:
                    p[f, x + 2, 16:24, :] = third(hi, lo, f)
                else:
                    r = 2 * k + f - 4
                    a, b = (rolled(mvhi, -r, 0), rolled(mvlo, 7 - r, 0))
                    p[f, x + 2, 16:24, :] = jnp.where(row < 4, a, b)
        return 0

    lax.fori_loop(0, n // 4, group, 0)
    for f in range(6):
        slot = 2 * f if f < 4 else 4 + f
        p[f, 1, 0:16, :], p[f, n + 2, 0:16, :] = picked(ends, idx, 0, rx0[slot], rx1[slot])
        if f < 4:
            p[f, 0, 0:16, :], p[f, n + 3, 0:16, :] = picked(ends, idx, 0, rx0[slot + 1], rx1[slot + 1])
        else:
            p[f, 0, 0:16, :] = jnp.zeros((16, 128), F32)
            p[f, n + 3, 0:16, :] = jnp.zeros((16, 128), F32)
        for e in (0, 1, n + 2, n + 3):
            p[f, e, 16:24, :] = zero


def wide(ref):
    return jnp.concatenate([ref[0], ref[1]], axis=1)


def ends_up(own, halo, slot):
    return jnp.where(slot == 1, up(own, 1), up(halo, 1))


def ends_down(own, halo, slot):
    return jnp.where(slot == 2, down(own, 1), down(halo, 1))


def ends_flow(k, f):
    kc, ku, kd = k
    fc, fu, fd = f
    fx = (kc + rolled(kc, -4, 1)) * (rolled(fc, -4, 1) - fc)
    fy = (kc + up(kc, 0)) * (up(fc, 0) - fc)
    flux = (fx - rolled(fx, 4, 1)) + (fy - down(fy, 0))
    return flux + ((kc + ku) * (fu - fc) - (kc + kd) * (fc - fd))


def to_ends(store, at, value, slot):
    value = jnp.where(slot == 1, up(value, 1), down(value, 1))
    store[at, 0] = value[:, 0:128]
    store[at, 1] = value[:, 128:256]


def edge(store, at, e, height=24):
    return pltpu.roll(store[at, e >> 5, 0:height, :], (126 - 4 * (e & 31)) & 127, 1)


def back(value, first, lane):
    return jnp.where(lane == 0, first, down(value, 1))


def inverse(cap):
    return DT * jnp.where(cap > 0, 1.0 / jnp.where(cap > 0, cap, 1.0), 0.0)


def forward(
    ends, idx, cw, p_in, t, rz0, rz1, re0, re1, mask, cls,
    p, v_out, h, a_out, later, later_z, r1, r2, tang, q_s, m, cs,
):
    n = r2.shape[0]
    for f in range(4):
        p[f, 1, 16:24, :], p[f, n + 2, 16:24, :] = picked(ends, idx, 0, re0[f], re1[f])

    slot = lanes((24, 256)) % 4
    own, halo = ([], [])
    for f in range(6):
        for col in range(2):
            lo, hi = picked(ends, idx, 2, rz0[f, col], rz1[f, col])
            h[f, col] = jnp.where(slot[:, 0:128] < 2, lo, hi)
        own.append(wide(t.at[f]))
        halo.append(wide(h.at[f]))
    near = [
        (halo[f], ends_up(own[f], halo[f], slot), ends_down(own[f], halo[f], slot)) for f in (0, 1, 2)
    ]
    vel, vel_down = (halo[5], ends_down(own[5], halo[5], slot))
    az = inverse(halo[3])
    qz = (1 / DT) * az * halo[4]
    rate = 0.5 * ends_flow(near[1], near[0]) + (vel_down * near[0][2] - vel * near[0][0])
    lz = near[0][0] + az * rate
    tz = az * (0.5 * ends_flow(near[2], near[0]) - qz * rate)
    later_z[0] = lz[:, 0:128]
    later_z[1] = lz[:, 128:256]
    for at, value in enumerate((halo[0], halo[1], halo[2], halo[5], lz, tz)):
        to_ends(m, at, value, slot)

    def make(e, _):
        a_out[e] = inverse(p[3, e])
        return 0

    lax.fori_loop(0, n + 4, make, 0, unroll=4)
    lane = lanes((24, 128))

    def first(t, carry):
        c0, d0, s0, fd, fs = carry
        e = t + 1
        c1, d1, s1 = (p[0, e + 1], p[1, e + 1], p[2, e + 1])
        ch, dh, sh, vh = (edge(m, k, e) for k in range(4))
        gx = c1 - c0
        fdx = (d0 + d1) * gx
        fsx = (s0 + s1) * gx
        gy = up(c0, 0) - c0
        fdy = (d0 + up(d0, 0)) * gy
        fsy = (s0 + up(s0, 0)) * gy
        gz = jnp.where(lane == 127, ch, up(c0, 1)) - c0
        fdz = (d0 + jnp.where(lane == 127, dh, up(d0, 1))) * gz
        fsz = (s0 + jnp.where(lane == 127, sh, up(s0, 1))) * gz
        gl = c0 - ch
        vc = p[5, e] * c0
        rate = (fdx - fd) + (fdy - down(fdy, 0)) + (fdz - back(fdz, (d0 + dh) * gl, lane))
        rate = 0.5 * rate + (back(vc, vh * ch, lane) - vc)
        other = (fsx - fs) + (fsy - down(fsy, 0)) + (fsz - back(fsz, (s0 + sh) * gl, lane))
        a = a_out[e]
        q = (1 / DT) * a * p[4, e]
        later[t] = c0 + a * rate
        tang[t] = a * (0.5 * other - q * rate)
        q_s[t] = q[0:16]
        r1[t] = rate[0:16]
        return c1, d1, s1, fdx, fsx

    c0, d0, s0 = (p[0, 0], p[1, 0], p[2, 0])
    c1, d1, s1 = (p[0, 1], p[1, 1], p[2, 1])
    start = (c1, d1, s1, (d0 + d1) * (c1 - c0), (s0 + s1) * (c1 - c0))
    lax.fori_loop(0, n + 2, first, start, unroll=U1)
    lane = lane[0:16]

    def second(x, carry):
        f1, f2, acc = carry
        t = x + 1
        e = t + 1
        l3, t3, d3, s3 = (later[t], tang[t], p[1, e], p[2, e])
        l0, t0, d0, s0 = (q[0:16] for q in (l3, t3, d3, s3))
        gl = later[t + 1, 0:16, :] - l0
        gt = tang[t + 1, 0:16, :] - t0
        dd = d0 + p[1, e + 1, 0:16, :]
        ss = s0 + p[2, e + 1, 0:16, :]
        fl = dd * gl
        ft = dd * gt + ss * gl
        dd = d3 + up(d3, 0)
        gly = up(l3, 0) - l3
        fly = dd * gly
        fty = dd * (up(t3, 0) - t3) + (s3 + up(s3, 0)) * gly
        dh, sh, vh, lh, th = (edge(m, k, e, 16) for k in (1, 2, 3, 4, 5))
        gl = jnp.where(lane == 127, lh, up(l0, 1)) - l0
        gt = jnp.where(lane == 127, th, up(t0, 1)) - t0
        dd = d0 + jnp.where(lane == 127, dh, up(d0, 1))
        ss = s0 + jnp.where(lane == 127, sh, up(s0, 1))
        flz = dd * gl
        ftz = dd * gt + ss * gl
        dd = d0 + dh
        gl = l0 - lh
        flb = back(flz, dd * gl, lane)
        ftb = back(ftz, dd * (t0 - th) + (s0 + sh) * gl, lane)
        vel = p[5, e, 0:16, :]
        vl = vel * l0
        vt = vel * t0
        rate = (fl - f1) + (fly - down(fly, 0))[0:16] + (flz - flb)
        rate = 0.5 * rate + (back(vl, vh * lh, lane) - vl)
        other = (ft - f2) + (fty - down(fty, 0))[0:16] + (ftz - ftb)
        other = 0.5 * other + (back(vt, vh * th, lane) - vt)
        final = t0 + a_out[e, 0:16, :] * (other - q_s[t] * rate)
        r2[x] = rate
        acc = jnp.where(x & 7 == 0, 0.0, acc) + final
        cs[x >> 3] = acc
        return fl, ft, acc

    gl = later[1, 0:16, :] - later[0, 0:16, :]
    gt = tang[1, 0:16, :] - tang[0, 0:16, :]
    dd = p[1, 1, 0:16, :] + p[1, 2, 0:16, :]
    ss = p[2, 1, 0:16, :] + p[2, 2, 0:16, :]
    lax.fori_loop(0, n, second, (dd * gl, dd * gt + ss * gl, jnp.zeros((16, 128), F32)), unroll=U2)

    lane8 = lanes((8, 128))
    row8 = rows((8, 128))
    expand = (
        lanes((16, 128)) // 8 == rows((16, 128))
    ).astype(F32)
    for yv in range(2):
        out = jnp.zeros((8, 128), F32)
        for X in range(n // 8):
            q = cs[X, 8 * yv : 8 * yv + 8, :]
            for k in (1, 2, 4):
                q = q + pltpu.roll(q, k, 0)
            for k in (1, 2, 4):
                q = q + jnp.where(lane8 & k == 0, pltpu.roll(q, 128 - k, 1), pltpu.roll(q, k, 1))
            out = jnp.where(row8 == X + 1, q, out)
        kind = cls[yv]
        weight = jnp.zeros(kind.shape, F32)
        for k in range(cw.shape[0]):
            weight = jnp.where(kind == k, cw[k], weight)
        weight = weight * mask[yv].astype(F32)
        spread = jnp.dot(weight, expand, precision=lax.Precision.HIGHEST, preferred_element_type=F32)
        v_out[yv] = out * spread * (1.0 / 512.0)


def merge(ends, idx, own, rx0, rx1, ry0, ry1, out, edge):
    row = rows((8, 128))
    for yv in range(2):
        lo, hi = picked(ends, idx, 0, rx0[yv], rx1[yv])
        value = jnp.where(row == 0, pltpu.roll(lo, 2, 0), own[yv])
        out[yv + 1] = jnp.where(row == 7, pltpu.roll(hi, 6, 0), value)
    lo = picked(ends, idx, 1, ry0[1], ry1[1])[0]
    hi = picked(ends, idx, 1, ry0[0], ry1[0])[1]
    for k, value in ((0, lo), (1, hi)):
        out[3 * k] = value
        edge[k] = value


def adjoint(
    ends, idx, vox, rz0, rz1, re0, re1, p, t, h, a_in, later, later_z, r1, r2,
    gd, gc, src, sc, sf, m,
):
    n = r2.shape[0]
    last = n // 8 + 1
    row = rows((8, 128))
    for X in range(last + 1):
        parts = []
        for yv in range(4):
            if X in (0, last) and yv in (0, 3):
                at, k = (last - 1 if X == 0 else 1, yv // 3)
                value = picked(ends, idx, 0, re0[k, at : at + 1, :], re1[k, at : at + 1, :])[X > 0]
            else:
                value = vox[yv, X : X + 1, :]
            parts.append(jnp.broadcast_to(value, (8, 128)))
        src[X, 0:8, :] = parts[1]
        src[X, 8:16, :] = parts[2]
        src[X, 16:24, :] = jnp.where(row < 4, parts[3], parts[0])

    slot8 = lanes((8, 128)) % 4
    sources = []
    for halo in (False, True):
        cols = []
        for col in range(2):
            here = (lanes((8, 128)) // 4 + 32 * col + 6) // 8 == row
            parts = []
            for yv in range(4):
                lo, hi = picked(ends, idx, 2, rz0[yv], rz1[yv]) if halo else (vox[yv], vox[yv])
                lo = jnp.broadcast_to(lo[:, 127:128], (8, 128))
                hi = jnp.broadcast_to(hi[:, 0:1], (8, 128))
                both = jnp.where(here, jnp.where(slot8 < 2, lo, hi), 0.0)
                for k in (1, 2, 4):
                    both = both + pltpu.roll(both, k, 0)
                parts.append(both)
            cols.append(
                jnp.concatenate([parts[1], parts[2], jnp.where(row < 4, parts[3], parts[0])], axis=0)
            )
        sources.append(jnp.concatenate(cols, axis=1))

    slot = lanes((24, 256)) % 4
    at, ah = (inverse(wide(t.at[3])), inverse(wide(h.at[3])))
    st, sh = (at * sources[0], ah * sources[1])
    dt, dh = (wide(t.at[1]), wide(h.at[1]))
    su = ends_up(st, sh, slot)
    flow = ends_flow(
        (dh, ends_up(dt, dh, slot), ends_down(dt, dh, slot)), (sh, su, ends_down(st, sh, slot))
    )
    fz = ah * (sources[1] + 0.5 * flow + wide(h.at[5]) * (su - sh))
    for k, value in enumerate((wide(h.at[0]), dh, sh, fz, wide(later_z))):
        to_ends(m, k, value, slot)

    def scale(e, _):
        sc[e] = a_in[e] * src[(e + 6) >> 3]
        return 0

    lax.fori_loop(0, n + 4, scale, 0, unroll=4)
    lane = lanes((24, 128))

    def third(t, f0):
        e = t + 1
        m0, d0 = (sc[e], p[1, e])
        dh, mh = (edge(m, 1, e), edge(m, 2, e))
        fx = (d0 + p[1, e + 1]) * (sc[e + 1] - m0)
        fy = (d0 + up(d0, 0)) * (up(m0, 0) - m0)
        gz = jnp.where(lane == 127, mh, up(m0, 1)) - m0
        fz = (d0 + jnp.where(lane == 127, dh, up(d0, 1))) * gz
        flow = (fx - f0) + (fy - down(fy, 0)) + (fz - back(fz, (d0 + dh) * (m0 - mh), lane))
        sf[t] = a_in[e] * (src[(e + 6) >> 3] + 0.5 * flow + p[5, e] * gz)
        return fx

    lax.fori_loop(0, n + 2, third, (p[1, 0] + p[1, 1]) * (sc[1] - sc[0]), unroll=U3)
    lane = lane[0:16]

    def fourth(x, e0):
        t = x + 1
        e = t + 1
        full = (sc[e], later[t], sf[t], p[0, e])
        m0, l0, s0, c0 = (q[0:16] for q in full)
        ex = (m0 - sc[e + 1, 0:16, :]) * (later[t + 1, 0:16, :] - l0)
        ex = ex + (s0 - sf[t + 1, 0:16, :]) * (p[0, e + 1, 0:16, :] - c0)
        m3, l3, s3, c3 = full
        ey = (m3 - up(m3, 0)) * (up(l3, 0) - l3) + (s3 - up(s3, 0)) * (up(c3, 0) - c3)
        ch, mh, sh, lh = (edge(m, k, e, 16) for k in (0, 2, 3, 4))
        mu, lu, su, cu = (
            jnp.where(lane == 127, b, up(a, 1)) for a, b in ((m0, mh), (l0, lh), (s0, sh), (c0, ch))
        )
        ez = (m0 - mu) * (lu - l0) + (s0 - su) * (cu - c0)
        eb = back(ez, (mh - m0) * (l0 - lh) + (sh - s0) * (c0 - ch), lane)
        gd[x] = 0.5 * ((ex + e0) + (ey + down(ey, 0))[0:16] + (ez + eb))
        gc[x] = (-1 / DT) * a_in[e, 0:16, :] * (m0 * r2[x] + s0 * r1[t])
        return ex

    ex = (sc[1, 0:16, :] - sc[2, 0:16, :]) * (later[1, 0:16, :] - later[0, 0:16, :])
    ex = ex + (sf[0, 0:16, :] - sf[1, 0:16, :]) * (p[0, 2, 0:16, :] - p[0, 1, 0:16, :])
    lax.fori_loop(0, n, fourth, ex, unroll=U4)


def coarse(x):
    x = jnp.transpose(x, (1, 0, 2))
    return jnp.pad(x, ((0, 0), (1, 1), (0, 0)))


def shards(c, d, s, cap, m, v, mask, cls, cw):
    n = c.shape[0]
    ends = [lax.axis_size(a) - 1 for a in ("gx", "gy", "gz")]
    idx = jnp.stack([lax.axis_index(a) for a in ("gx", "gy", "gz")]).astype(jnp.int32)
    fields = [pltpu.with_memory_space_constraint(f, pltpu.HBM) for f in (c, d, s, cap, m, v)]
    all_f, bx0, bx1, by0, by1, ys0, ys1 = call(
        pack_a,
        [(6, n, 16, 128)] + [(10, 16, 128)] * 2 + [(n + n // 4, 8, 128)] * 2 + [(6, 8, 128)] * 2,
        [SM] + [HB] * 6,
        (idx, *fields),
        [pltpu.SemaphoreType.DMA((6,))],
    )
    ys1 = swap(ys1, "gy", 1)
    ys0 = swap(ys0, "gy", 0)
    ry1 = swap(by1, "gy", 1)
    ry0 = swap(by0, "gy", 0)
    rx0 = swap(bx0, "gx", 0)
    rx1 = swap(bx1, "gx", 1)
    (tm,) = call(pack_t, [(6, 2, 16, 128)], [VM], (all_f,))
    t, e0, e1 = call(
        partial(pack_b, ends, n),
        [(6, 2, 24, 128), (4, 8, 128), (4, 8, 128)],
        [SM] + [VM] * 5,
        (idx, tm, rx0, rx1, ys0, ys1),
    )
    (p,) = call(
        partial(pack_c, ends),
        [(6, n + 4, 24, 128)],
        [SM] + [VM] * 5,
        (idx, all_f, rx0, rx1, ry0, ry1),
    )
    rz1 = swap(t, "gz", 1)
    rz0 = swap(t, "gz", 0)
    re0 = swap(e0, "gx", 0)
    re1 = swap(e1, "gx", 1)
    p, vox, h, a, later, later_z, r1, r2 = call(
        partial(forward, ends),
        [
            (6, n + 4, 24, 128),
            (2, 8, 128),
            (6, 2, 24, 128),
            (n + 4, 24, 128),
            (n + 2, 24, 128),
            (2, 24, 128),
            (n + 2, 16, 128),
            (n, 16, 128),
        ],
        [SM, SM] + [VM] * 8,
        (idx, cw, p, t, rz0, rz1, re0, re1, coarse(mask), coarse(cls)),
        [
            pltpu.VMEM((n + 2, 24, 128), F32),
            pltpu.VMEM((n + 2, 16, 128), F32),
            pltpu.VMEM((6, 2, 24, 128), F32),
            pltpu.VMEM((n // 8, 16, 128), F32),
        ],
        alias={2: 0},
    )
    ry1 = swap(vox, "gy", 1)
    ry0 = swap(vox, "gy", 0)
    rx0 = swap(vox, "gx", 0)
    rx1 = swap(vox, "gx", 1)
    vox, edge = call(
        partial(merge, ends), [(4, 8, 128), (2, 8, 128)], [SM] + [VM] * 5, (idx, vox, rx0, rx1, ry0, ry1), limit=1
    )
    rz1 = swap(vox, "gz", 1)
    rz0 = swap(vox, "gz", 0)
    re0 = swap(edge, "gx", 0)
    re1 = swap(edge, "gx", 1)
    gd, gc = call(
        partial(adjoint, ends),
        [(n, 16, 128)] * 2,
        [SM] + [VM] * 13,
        (idx, vox, rz0, rz1, re0, re1, p, t, h, a, later, later_z, r1, r2),
        [
            pltpu.VMEM((n // 8 + 2, 24, 128), F32),
            pltpu.VMEM((n + 4, 24, 128), F32),
            pltpu.VMEM((n + 2, 24, 128), F32),
            pltpu.VMEM((5, 2, 24, 128), F32),
        ],
    )
    return gd, gc


def solution(mesh):
    spec = P("gx", "gy", "gz")
    return jax.shard_map(
        shards, mesh=mesh, in_specs=(spec,) * 8 + (P(),), out_specs=(spec, spec), check_vma=False
    )
```

```python
from functools import partial

import jax
import jax.numpy as jnp
from jax import lax
from jax.experimental import pallas as pl
from jax.experimental.pallas import tpu as pltpu
from jax.sharding import PartitionSpec as P


DT = 0.1
CHUNKS = 1
U1, U2, U3, U4 = (5, 4, 10, 8)
F32 = jnp.float32
VM = pl.BlockSpec(memory_space=pltpu.VMEM)
SM = pl.BlockSpec(memory_space=pltpu.SMEM)
HB = pl.BlockSpec(memory_space=pltpu.HBM)


def swap_pairs(size, first, ends=True):
    pairs = []
    for i in range(first, size if ends else size - 1, 2):
        pairs += [(i, (i + 1) % size), ((i + 1) % size, i)]
    return pairs


def swap(value, axis, first, name):
    ends = name not in PARTIAL
    return lax.ppermute(value, axis, swap_pairs(lax.axis_size(axis), first, ends))


PARTIAL = ()


def call(body, outs, specs, args, scratch=(), limit=24, alias=None):
    return pl.pallas_call(
        body,
        out_shape=[jax.ShapeDtypeStruct(s, F32) for s in outs],
        in_specs=specs,
        out_specs=[VM] * len(outs),
        scratch_shapes=list(scratch),
        input_output_aliases=alias or {},
        compiler_params=pltpu.CompilerParams(vmem_limit_bytes=limit << 20),
    )(*args)


def rows(shape):
    return lax.broadcasted_iota(jnp.int32, shape, len(shape) - 2)


def lanes(shape):
    return lax.broadcasted_iota(jnp.int32, shape, len(shape) - 1)


def up(x, axis):
    return pltpu.roll(x, x.shape[axis] - 1, axis)


def down(x, axis):
    return pltpu.roll(x, 1, axis)


def rolled(x, shift, axis):
    shift = shift % x.shape[axis]
    return x if shift == 0 else pltpu.roll(x, shift, axis)


def is_even(idx, axis):
    return idx[axis] % 2 == 0


def picked(ends, idx, axis, r0, r1):
    even = is_even(idx, axis)
    lo = jnp.where(even, r1, r0)
    hi = jnp.where(even, r0, r1)
    return jnp.where(idx[axis] > 0, lo, 0.0), jnp.where(idx[axis] < ends[axis], hi, 0.0)


def pack_a(idx, c, d, s, cap, m, v, all_f, bx0, bx1, by0, by1, ys0, ys1, sems):
    n = c.shape[0]
    xeven = is_even(idx, 0)
    yeven = is_even(idx, 1)
    row = rows((8, 128))
    part = n // CHUNKS
    copies = [
        pltpu.make_async_copy(
            ref.at[pl.ds(k * part, part)], all_f.at[f, pl.ds(k * part, part)], sems.at[f * CHUNKS + k]
        )
        for k in range(CHUNKS)
        for f, ref in enumerate((c, d, s, cap, m, v))
    ]
    for copy in copies:
        copy.start()
    for copy in copies:
        copy.wait()
    for out, hi in ((bx0, xeven), (bx1, jnp.logical_not(xeven))):
        one = jnp.where(hi, n - 1, 0)
        two = jnp.where(hi, n - 2, 1)
        for slot, (f, at) in enumerate(
            [(f, i) for f in range(4) for i in (one, two)] + [(4, one), (5, one)]
        ):
            out[slot] = all_f[f, at]

    def tiles(four, low):
        out = None
        for f, value in enumerate(four):
            part = rolled(value, 2 * f if low else 2 * f + 2, 0)
            out = part if f == 0 else jnp.where(row < 2 * f, out, part)
        return out

    def put(at, lo, hi):
        by0[at] = jnp.where(yeven, hi, lo)
        by1[at] = jnp.where(yeven, lo, hi)

    def group(g, _):
        lo = hi = None
        for k in range(8):
            x = g * 4 + k // 2
            if k % 2 == 0:
                put(
                    x,
                    tiles([all_f[f, x, 0:8, :] for f in range(4)], True),
                    tiles([all_f[f, x, 8:16, :] for f in range(4)], False),
                )
            a = rolled(all_f[4 + k % 2, x, 0:8, :], k, 0)
            b = rolled(all_f[4 + k % 2, x, 8:16, :], k + 1, 0)
            lo = a if k == 0 else jnp.where(row < k, lo, a)
            hi = b if k == 0 else jnp.where(row < k, hi, b)
        put(n + g, lo, hi)
        return 0

    lax.fori_loop(0, n // 4, group, 0, unroll=2)
    lane = lanes((8, 128))
    for ys in (ys0, ys1):
        ys[0:4] = jnp.zeros((4, 8, 128), F32)
    for ys, by in ((ys0, by0), (ys1, by1)):
        ys[4] = by[0]
        ys[5] = by[n - 1]

    def ends_of(g, _):
        out = [None] * 4
        for k in range(8):
            x = g * 8 + k
            parts = (by0[x], by1[x], all_f[5, x, 0:8, :], all_f[5, x, 8:16, :])
            for i, value in enumerate(parts):
                part = rolled(value, 4 * k + 2, 1)
                out[i] = part if k == 0 else jnp.where(lane < 4 * k, out[i], part)
        at = g * 32 + 8
        for col in range(2):
            shift = (at - 128 * col) & 127
            here = (lane + 128 * col >= at) & (lane + 128 * col < at + 32)
            one, two, low, high = (pltpu.roll(q, shift, 1) for q in out)
            v0 = jnp.where(yeven, high, low)
            v1 = jnp.where(yeven, low, high)
            for ys, i, value in ((ys0, 0, one), (ys1, 0, two), (ys0, 2, v0), (ys1, 2, v1)):
                ys[i + col] = jnp.where(here, value, ys[i + col])
        return 0

    lax.fori_loop(0, n // 8, ends_of, 0, unroll=2)


def pack_t(all_f, t):
    n = all_f.shape[1]
    lane = lanes((16, 128))
    t[...] = jnp.zeros(t.shape, F32)

    def pack(g, _):
        at = g * 32 + 8
        for f in range(6):
            out = None
            for k in range(8):
                part = rolled(all_f[f, g * 8 + k], 4 * k + 2, 1)
                out = part if k == 0 else jnp.where(lane < 4 * k, out, part)
            out = pltpu.roll(out, at & 127, 1)
            for col in range(2):
                here = (lane + 128 * col >= at) & (lane + 128 * col < at + 32)
                t[f, col] = jnp.where(here, out, t[f, col])
        return 0

    lax.fori_loop(0, n // 8, pack, 0)


def third(hi, lo, f):
    row = rows((8, 128))
    return jnp.where(row < 4, rolled(hi, -2 * f, 0), rolled(lo, 6 - 2 * f, 0))


def pack_b(ends, planes, idx, tm, rx0, rx1, ys0, ys1, t, b0, b1, e0, e1):
    xeven = is_even(idx, 0)
    zeven = is_even(idx, 2)
    left = lanes((24, 128)) % 4 < 2
    row = rows((8, 128))
    lane = lanes((16, 128))
    tiles = [picked(ends, idx, 1, ys0[k], ys1[k]) for k in range(6)]
    for f in range(6):
        halo = picked(ends, idx, 0, rx0[2 * f if f < 4 else 4 + f], rx1[2 * f if f < 4 else 4 + f])
        for col in range(2):
            at = (1, planes + 2)[col]
            part = rolled(halo[col], 4 * at + 2, 1)
            t[f, col, 0:16, :] = jnp.where(lane // 4 == at % 32, part, tm[f, col])
            if f < 4:
                t[f, col, 16:24, :] = third(tiles[col][1], tiles[col][0], f)
            elif f == 4:
                t[f, col, 16:24, :] = jnp.zeros((8, 128), F32)
            else:
                t[f, col, 16:24, :] = jnp.where(row < 4, tiles[2 + col][1], tiles[2 + col][0])
        one, two = (t[f, 0], t[f, 1])
        hi = jnp.where(left, one, pltpu.roll(two, 2, 1))
        lo = jnp.where(left, pltpu.roll(one, 126, 1), two)
        b0[f] = jnp.where(zeven, hi, lo)
        b1[f] = jnp.where(zeven, lo, hi)
    for f in range(4):
        lo, hi = (third(tiles[k][1], tiles[k][0], f) for k in (4, 5))
        e0[f] = jnp.where(xeven, hi, lo)
        e1[f] = jnp.where(xeven, lo, hi)


def pack_c(ends, idx, all_f, rx0, rx1, ry0, ry1, p, a_out):
    n = all_f.shape[1]
    row = rows((8, 128))
    zero = jnp.zeros((8, 128), F32)

    def both(at):
        return picked(ends, idx, 1, ry0[at], ry1[at])

    def group(g, _):
        mvlo, mvhi = both(n + g)
        for k in range(4):
            x = g * 4 + k
            lo, hi = both(x)
            for f in range(6):
                p[f, x + 2, 0:16, :] = all_f[f, x]
                if f < 4:
                    p[f, x + 2, 16:24, :] = third(hi, lo, f)
                else:
                    r = 2 * k + f - 4
                    a, b = (rolled(mvhi, -r, 0), rolled(mvlo, 7 - r, 0))
                    p[f, x + 2, 16:24, :] = jnp.where(row < 4, a, b)
        return 0

    lax.fori_loop(0, n // 4, group, 0)
    for f in range(6):
        slot = 2 * f if f < 4 else 4 + f
        p[f, 1, 0:16, :], p[f, n + 2, 0:16, :] = picked(ends, idx, 0, rx0[slot], rx1[slot])
        if f < 4:
            p[f, 0, 0:16, :], p[f, n + 3, 0:16, :] = picked(ends, idx, 0, rx0[slot + 1], rx1[slot + 1])
        else:
            p[f, 0, 0:16, :] = jnp.zeros((16, 128), F32)
            p[f, n + 3, 0:16, :] = jnp.zeros((16, 128), F32)
        for e in (0, 1, n + 2, n + 3):
            p[f, e, 16:24, :] = zero

    def make(e, _):
        a_out[e] = inverse(p[3, e])
        return 0

    lax.fori_loop(0, n + 4, make, 0, unroll=4)


def wide(ref):
    return jnp.concatenate([ref[0], ref[1]], axis=1)


def ends_up(own, halo, slot):
    return jnp.where(slot == 1, up(own, 1), up(halo, 1))


def ends_down(own, halo, slot):
    return jnp.where(slot == 2, down(own, 1), down(halo, 1))


def ends_flow(k, f):
    kc, ku, kd = k
    fc, fu, fd = f
    fx = (kc + rolled(kc, -4, 1)) * (rolled(fc, -4, 1) - fc)
    fy = (kc + up(kc, 0)) * (up(fc, 0) - fc)
    flux = (fx - rolled(fx, 4, 1)) + (fy - down(fy, 0))
    return flux + ((kc + ku) * (fu - fc) - (kc + kd) * (fc - fd))


def to_ends(store, at, value, slot):
    value = jnp.where(slot == 1, up(value, 1), down(value, 1))
    store[at, 0] = value[:, 0:128]
    store[at, 1] = value[:, 128:256]


def edge(store, at, e, height=24):
    return pltpu.roll(store[at, e >> 5, 0:height, :], (126 - 4 * (e & 31)) & 127, 1)


def back(value, first, lane):
    return jnp.where(lane == 0, first, down(value, 1))


def inverse(cap):
    return DT * jnp.where(cap > 0, 1.0 / jnp.where(cap > 0, cap, 1.0), 0.0)


def forward(
    ends, idx, cw, p_in, a_in, t, rz0, rz1, re0, re1, mask, cls,
    p, v_out, h, a_out, later, later_z, r1, r2, tang, q_s, m, cs,
):
    n = r2.shape[0]
    for f in range(4):
        p[f, 1, 16:24, :], p[f, n + 2, 16:24, :] = picked(ends, idx, 0, re0[f], re1[f])
    for e in (1, n + 2):
        a_out[e, 16:24, :] = inverse(p[3, e, 16:24, :])

    slot = lanes((24, 256)) % 4
    own, halo = ([], [])
    for f in range(6):
        lo, hi = picked(ends, idx, 2, rz0[f], rz1[f])
        h[f, 0] = jnp.where(slot[:, 0:128] < 2, lo, pltpu.roll(hi, 2, 1))
        h[f, 1] = jnp.where(slot[:, 0:128] < 2, pltpu.roll(lo, 126, 1), hi)
        own.append(wide(t.at[f]))
        halo.append(wide(h.at[f]))
    near = [
        (halo[f], ends_up(own[f], halo[f], slot), ends_down(own[f], halo[f], slot)) for f in (0, 1, 2)
    ]
    vel, vel_down = (halo[5], ends_down(own[5], halo[5], slot))
    az = inverse(halo[3])
    qz = (1 / DT) * az * halo[4]
    rate = 0.5 * ends_flow(near[1], near[0]) + (vel_down * near[0][2] - vel * near[0][0])
    lz = near[0][0] + az * rate
    tz = az * (0.5 * ends_flow(near[2], near[0]) - qz * rate)
    later_z[0] = lz[:, 0:128]
    later_z[1] = lz[:, 128:256]
    for at, value in enumerate((halo[0], halo[1], halo[2], halo[5], lz, tz)):
        to_ends(m, at, value, slot)

    lane = lanes((24, 128))

    def first(t, carry):
        c0, d0, s0, fd, fs = carry
        e = t + 1
        c1, d1, s1 = (p[0, e + 1], p[1, e + 1], p[2, e + 1])
        ch, dh, sh, vh = (edge(m, k, e) for k in range(4))
        gx = c1 - c0
        fdx = (d0 + d1) * gx
        fsx = (s0 + s1) * gx
        gy = up(c0, 0) - c0
        fdy = (d0 + up(d0, 0)) * gy
        fsy = (s0 + up(s0, 0)) * gy
        gz = jnp.where(lane == 127, ch, up(c0, 1)) - c0
        fdz = (d0 + jnp.where(lane == 127, dh, up(d0, 1))) * gz
        fsz = (s0 + jnp.where(lane == 127, sh, up(s0, 1))) * gz
        gl = c0 - ch
        vc = p[5, e] * c0
        rate = (fdx - fd) + (fdy - down(fdy, 0)) + (fdz - back(fdz, (d0 + dh) * gl, lane))
        rate = 0.5 * rate + (back(vc, vh * ch, lane) - vc)
        other = (fsx - fs) + (fsy - down(fsy, 0)) + (fsz - back(fsz, (s0 + sh) * gl, lane))
        a = a_out[e]
        q = (1 / DT) * a * p[4, e]
        later[t] = c0 + a * rate
        tang[t] = a * (0.5 * other - q * rate)
        q_s[t] = q[0:16]
        r1[t] = rate[0:16]
        return c1, d1, s1, fdx, fsx

    c0, d0, s0 = (p[0, 0], p[1, 0], p[2, 0])
    c1, d1, s1 = (p[0, 1], p[1, 1], p[2, 1])
    start = (c1, d1, s1, (d0 + d1) * (c1 - c0), (s0 + s1) * (c1 - c0))
    lax.fori_loop(0, n + 2, first, start, unroll=U1)
    lane = lane[0:16]

    def second(x, carry):
        f1, f2, acc = carry
        t = x + 1
        e = t + 1
        l3, t3, d3, s3 = (later[t], tang[t], p[1, e], p[2, e])
        l0, t0, d0, s0 = (q[0:16] for q in (l3, t3, d3, s3))
        gl = later[t + 1, 0:16, :] - l0
        gt = tang[t + 1, 0:16, :] - t0
        dd = d0 + p[1, e + 1, 0:16, :]
        ss = s0 + p[2, e + 1, 0:16, :]
        fl = dd * gl
        ft = dd * gt + ss * gl
        dd = d3 + up(d3, 0)
        gly = up(l3, 0) - l3
        fly = dd * gly
        fty = dd * (up(t3, 0) - t3) + (s3 + up(s3, 0)) * gly
        dh, sh, vh, lh, th = (edge(m, k, e, 16) for k in (1, 2, 3, 4, 5))
        gl = jnp.where(lane == 127, lh, up(l0, 1)) - l0
        gt = jnp.where(lane == 127, th, up(t0, 1)) - t0
        dd = d0 + jnp.where(lane == 127, dh, up(d0, 1))
        ss = s0 + jnp.where(lane == 127, sh, up(s0, 1))
        flz = dd * gl
        ftz = dd * gt + ss * gl
        dd = d0 + dh
        gl = l0 - lh
        flb = back(flz, dd * gl, lane)
        ftb = back(ftz, dd * (t0 - th) + (s0 + sh) * gl, lane)
        vel = p[5, e, 0:16, :]
        vl = vel * l0
        vt = vel * t0
        rate = (fl - f1) + (fly - down(fly, 0))[0:16] + (flz - flb)
        rate = 0.5 * rate + (back(vl, vh * lh, lane) - vl)
        other = (ft - f2) + (fty - down(fty, 0))[0:16] + (ftz - ftb)
        other = 0.5 * other + (back(vt, vh * th, lane) - vt)
        final = t0 + a_out[e, 0:16, :] * (other - q_s[t] * rate)
        r2[x] = rate
        acc = jnp.where(x & 7 == 0, 0.0, acc) + final
        cs[x >> 3] = acc
        return fl, ft, acc

    gl = later[1, 0:16, :] - later[0, 0:16, :]
    gt = tang[1, 0:16, :] - tang[0, 0:16, :]
    dd = p[1, 1, 0:16, :] + p[1, 2, 0:16, :]
    ss = p[2, 1, 0:16, :] + p[2, 2, 0:16, :]
    lax.fori_loop(0, n, second, (dd * gl, dd * gt + ss * gl, jnp.zeros((16, 128), F32)), unroll=U2)

    lane8 = lanes((8, 128))
    row8 = rows((8, 128))
    expand = (
        lanes((16, 128)) // 8 == rows((16, 128))
    ).astype(F32)
    for yv in range(2):
        out = jnp.zeros((8, 128), F32)
        for X in range(n // 8):
            q = cs[X, 8 * yv : 8 * yv + 8, :]
            for k in (1, 2, 4):
                q = q + pltpu.roll(q, k, 0)
            for k in (1, 2, 4):
                q = q + jnp.where(lane8 & k == 0, pltpu.roll(q, 128 - k, 1), pltpu.roll(q, k, 1))
            out = jnp.where(row8 == X + 1, q, out)
        kind = cls[yv]
        weight = jnp.zeros(kind.shape, F32)
        for k in range(cw.shape[0]):
            weight = jnp.where(kind == k, cw[k], weight)
        weight = weight * mask[yv].astype(F32)
        spread = jnp.dot(weight, expand, precision=lax.Precision.HIGHEST, preferred_element_type=F32)
        v_out[yv] = out * spread * (1.0 / 512.0)


def merge(ends, idx, own, rx0, rx1, ry0, ry1, out, edge):
    row = rows((8, 128))
    for yv in range(2):
        lo, hi = picked(ends, idx, 0, rx0[yv], rx1[yv])
        value = jnp.where(row == 0, pltpu.roll(lo, 2, 0), own[yv])
        out[yv + 1] = jnp.where(row == 7, pltpu.roll(hi, 6, 0), value)
    lo = picked(ends, idx, 1, ry0[1], ry1[1])[0]
    hi = picked(ends, idx, 1, ry0[0], ry1[0])[1]
    for k, value in ((0, lo), (1, hi)):
        out[3 * k] = value
        edge[k] = value


def adjoint(
    ends, idx, vox, rz0, rz1, re0, re1, p, t, h, a_in, later, later_z, r1, r2,
    gd, gc, src, sc, sf, m,
):
    n = r2.shape[0]
    last = n // 8 + 1
    row = rows((8, 128))
    for X in range(last + 1):
        parts = []
        for yv in range(4):
            if X in (0, last) and yv in (0, 3):
                at, k = (last - 1 if X == 0 else 1, yv // 3)
                value = picked(ends, idx, 0, re0[k, at : at + 1, :], re1[k, at : at + 1, :])[X > 0]
            else:
                value = vox[yv, X : X + 1, :]
            parts.append(jnp.broadcast_to(value, (8, 128)))
        src[X, 0:8, :] = parts[1]
        src[X, 8:16, :] = parts[2]
        src[X, 16:24, :] = jnp.where(row < 4, parts[3], parts[0])

    slot8 = lanes((8, 128)) % 4
    sources = []
    for halo in (False, True):
        cols = []
        for col in range(2):
            here = (lanes((8, 128)) // 4 + 32 * col + 6) // 8 == row
            parts = []
            for yv in range(4):
                lo, hi = picked(ends, idx, 2, rz0[yv], rz1[yv]) if halo else (vox[yv], vox[yv])
                lo = jnp.broadcast_to(lo[:, 127:128], (8, 128))
                hi = jnp.broadcast_to(hi[:, 0:1], (8, 128))
                both = jnp.where(here, jnp.where(slot8 < 2, lo, hi), 0.0)
                for k in (1, 2, 4):
                    both = both + pltpu.roll(both, k, 0)
                parts.append(both)
            cols.append(
                jnp.concatenate([parts[1], parts[2], jnp.where(row < 4, parts[3], parts[0])], axis=0)
            )
        sources.append(jnp.concatenate(cols, axis=1))

    slot = lanes((24, 256)) % 4
    at, ah = (inverse(wide(t.at[3])), inverse(wide(h.at[3])))
    st, sh = (at * sources[0], ah * sources[1])
    dt, dh = (wide(t.at[1]), wide(h.at[1]))
    su = ends_up(st, sh, slot)
    flow = ends_flow(
        (dh, ends_up(dt, dh, slot), ends_down(dt, dh, slot)), (sh, su, ends_down(st, sh, slot))
    )
    fz = ah * (sources[1] + 0.5 * flow + wide(h.at[5]) * (su - sh))
    for k, value in enumerate((wide(h.at[0]), dh, sh, fz, wide(later_z))):
        to_ends(m, k, value, slot)

    def scale(e, _):
        sc[e] = a_in[e] * src[(e + 6) >> 3]
        return 0

    lax.fori_loop(0, n + 4, scale, 0, unroll=4)
    lane = lanes((24, 128))

    def third(t, f0):
        e = t + 1
        m0, d0 = (sc[e], p[1, e])
        dh, mh = (edge(m, 1, e), edge(m, 2, e))
        fx = (d0 + p[1, e + 1]) * (sc[e + 1] - m0)
        fy = (d0 + up(d0, 0)) * (up(m0, 0) - m0)
        gz = jnp.where(lane == 127, mh, up(m0, 1)) - m0
        fz = (d0 + jnp.where(lane == 127, dh, up(d0, 1))) * gz
        flow = (fx - f0) + (fy - down(fy, 0)) + (fz - back(fz, (d0 + dh) * (m0 - mh), lane))
        sf[t] = a_in[e] * (src[(e + 6) >> 3] + 0.5 * flow + p[5, e] * gz)
        return fx

    lax.fori_loop(0, n + 2, third, (p[1, 0] + p[1, 1]) * (sc[1] - sc[0]), unroll=U3)
    lane = lane[0:16]

    def fourth(x, e0):
        t = x + 1
        e = t + 1
        full = (sc[e], later[t], sf[t], p[0, e])
        m0, l0, s0, c0 = (q[0:16] for q in full)
        ex = (m0 - sc[e + 1, 0:16, :]) * (later[t + 1, 0:16, :] - l0)
        ex = ex + (s0 - sf[t + 1, 0:16, :]) * (p[0, e + 1, 0:16, :] - c0)
        m3, l3, s3, c3 = full
        ey = (m3 - up(m3, 0)) * (up(l3, 0) - l3) + (s3 - up(s3, 0)) * (up(c3, 0) - c3)
        ch, mh, sh, lh = (edge(m, k, e, 16) for k in (0, 2, 3, 4))
        mu, lu, su, cu = (
            jnp.where(lane == 127, b, up(a, 1)) for a, b in ((m0, mh), (l0, lh), (s0, sh), (c0, ch))
        )
        ez = (m0 - mu) * (lu - l0) + (s0 - su) * (cu - c0)
        eb = back(ez, (mh - m0) * (l0 - lh) + (sh - s0) * (c0 - ch), lane)
        gd[x] = 0.5 * ((ex + e0) + (ey + down(ey, 0))[0:16] + (ez + eb))
        gc[x] = (-1 / DT) * a_in[e, 0:16, :] * (m0 * r2[x] + s0 * r1[t])
        return ex

    ex = (sc[1, 0:16, :] - sc[2, 0:16, :]) * (later[1, 0:16, :] - later[0, 0:16, :])
    ex = ex + (sf[0, 0:16, :] - sf[1, 0:16, :]) * (p[0, 2, 0:16, :] - p[0, 1, 0:16, :])
    lax.fori_loop(0, n, fourth, ex, unroll=U4)


def coarse(x):
    x = jnp.transpose(x, (1, 0, 2))
    return jnp.pad(x, ((0, 0), (1, 1), (0, 0)))


def shards(c, d, s, cap, m, v, mask, cls, cw):
    n = c.shape[0]
    ends = [lax.axis_size(a) - 1 for a in ("gx", "gy", "gz")]
    idx = jnp.stack([lax.axis_index(a) for a in ("gx", "gy", "gz")]).astype(jnp.int32)
    fields = [pltpu.with_memory_space_constraint(f, pltpu.HBM) for f in (c, d, s, cap, m, v)]
    all_f, bx0, bx1, by0, by1, ys0, ys1 = call(
        pack_a,
        [(6, n, 16, 128)] + [(10, 16, 128)] * 2 + [(n + n // 4, 8, 128)] * 2 + [(6, 8, 128)] * 2,
        [SM] + [HB] * 6,
        (idx, *fields),
        [pltpu.SemaphoreType.DMA((6 * CHUNKS,))],
    )
    ys1 = swap(ys1, "gy", 1, "small_y1")
    ys0 = swap(ys0, "gy", 0, "small_y0")
    ry1 = swap(by1, "gy", 1, "large_y1")
    ry0 = swap(by0, "gy", 0, "large_y0")
    rx0 = swap(bx0, "gx", 0, "face_x0")
    rx1 = swap(bx1, "gx", 1, "face_x1")
    (tm,) = call(pack_t, [(6, 2, 16, 128)], [VM], (all_f,))
    t, bz0, bz1, e0, e1 = call(
        partial(pack_b, ends, n),
        [(6, 2, 24, 128), (6, 24, 128), (6, 24, 128), (4, 8, 128), (4, 8, 128)],
        [SM] + [VM] * 5,
        (idx, tm, rx0, rx1, ys0, ys1),
    )
    p, a = call(
        partial(pack_c, ends),
        [(6, n + 4, 24, 128), (n + 4, 24, 128)],
        [SM] + [VM] * 5,
        (idx, all_f, rx0, rx1, ry0, ry1),
    )
    rz1 = swap(bz1, "gz", 1, "ends_z1")
    rz0 = swap(bz0, "gz", 0, "ends_z0")
    re0 = swap(e0, "gx", 0, "rows_x0")
    re1 = swap(e1, "gx", 1, "rows_x1")
    p, vox, h, a, later, later_z, r1, r2 = call(
        partial(forward, ends),
        [
            (6, n + 4, 24, 128),
            (2, 8, 128),
            (6, 2, 24, 128),
            (n + 4, 24, 128),
            (n + 2, 24, 128),
            (2, 24, 128),
            (n + 2, 16, 128),
            (n, 16, 128),
        ],
        [SM, SM] + [VM] * 9,
        (idx, cw, p, a, t, rz0, rz1, re0, re1, coarse(mask), coarse(cls)),
        [
            pltpu.VMEM((n + 2, 24, 128), F32),
            pltpu.VMEM((n + 2, 16, 128), F32),
            pltpu.VMEM((6, 2, 24, 128), F32),
            pltpu.VMEM((n // 8, 16, 128), F32),
        ],
        alias={2: 0, 3: 3},
    )
    ry1 = swap(vox, "gy", 1, "voxel_y1")
    ry0 = swap(vox, "gy", 0, "voxel_y0")
    rx0 = swap(vox, "gx", 0, "voxel_x0")
    rx1 = swap(vox, "gx", 1, "voxel_x1")
    vox, edge = call(
        partial(merge, ends), [(4, 8, 128), (2, 8, 128)], [SM] + [VM] * 5, (idx, vox, rx0, rx1, ry0, ry1), limit=1
    )
    rz1 = swap(vox, "gz", 1, "voxel_z1")
    rz0 = swap(vox, "gz", 0, "voxel_z0")
    re0 = swap(edge, "gx", 0, "corner_x0")
    re1 = swap(edge, "gx", 1, "corner_x1")
    gd, gc = call(
        partial(adjoint, ends),
        [(n, 16, 128)] * 2,
        [SM] + [VM] * 13,
        (idx, vox, rz0, rz1, re0, re1, p, t, h, a, later, later_z, r1, r2),
        [
            pltpu.VMEM((n // 8 + 2, 24, 128), F32),
            pltpu.VMEM((n + 4, 24, 128), F32),
            pltpu.VMEM((n + 2, 24, 128), F32),
            pltpu.VMEM((5, 2, 24, 128), F32),
        ],
    )
    return gd, gc


def solution(mesh):
    spec = P("gx", "gy", "gz")
    return jax.shard_map(
        shards, mesh=mesh, in_specs=(spec,) * 8 + (P(),), out_specs=(spec, spec), check_vma=False
    )
```

```python
from functools import partial

import jax
import jax.numpy as jnp
from jax import lax
from jax.experimental import pallas as pl
from jax.experimental.pallas import tpu as pltpu
from jax.sharding import PartitionSpec as P


DT = 0.1
CHUNKS = 1
U1, U2, U3, U4 = (5, 4, 8, 8)
F32 = jnp.float32
VM = pl.BlockSpec(memory_space=pltpu.VMEM)
SM = pl.BlockSpec(memory_space=pltpu.SMEM)
HB = pl.BlockSpec(memory_space=pltpu.HBM)


def swap_pairs(size, first, ends=True):
    pairs = []
    for i in range(first, size if ends else size - 1, 2):
        pairs += [(i, (i + 1) % size), ((i + 1) % size, i)]
    return pairs


def swap(value, axis, first, name):
    ends = name not in PARTIAL
    return lax.ppermute(value, axis, swap_pairs(lax.axis_size(axis), first, ends))


PARTIAL = ()


def call(body, outs, specs, args, scratch=(), limit=24, alias=None, hbm=0):
    return pl.pallas_call(
        body,
        out_shape=[jax.ShapeDtypeStruct(s, F32) for s in outs],
        in_specs=specs,
        out_specs=[HB] * hbm + [VM] * (len(outs) - hbm),
        scratch_shapes=list(scratch),
        input_output_aliases=alias or {},
        compiler_params=pltpu.CompilerParams(vmem_limit_bytes=limit << 20),
    )(*args)


def rows(shape):
    return lax.broadcasted_iota(jnp.int32, shape, len(shape) - 2)


def lanes(shape):
    return lax.broadcasted_iota(jnp.int32, shape, len(shape) - 1)


def up(x, axis):
    return pltpu.roll(x, x.shape[axis] - 1, axis)


def down(x, axis):
    return pltpu.roll(x, 1, axis)


def rolled(x, shift, axis):
    shift = shift % x.shape[axis]
    return x if shift == 0 else pltpu.roll(x, shift, axis)


def is_even(idx, axis):
    return idx[axis] % 2 == 0


def picked(ends, idx, axis, r0, r1):
    even = is_even(idx, axis)
    lo = jnp.where(even, r1, r0)
    hi = jnp.where(even, r0, r1)
    return jnp.where(idx[axis] > 0, lo, 0.0), jnp.where(idx[axis] < ends[axis], hi, 0.0)


def pack_a(idx, c, d, s, cap, m, v, all_f, bx0, bx1, by0, by1, ys0, ys1, sems):
    n = c.shape[0]
    xeven = is_even(idx, 0)
    yeven = is_even(idx, 1)
    row = rows((8, 128))
    part = n // CHUNKS
    copies = [
        pltpu.make_async_copy(
            ref.at[pl.ds(k * part, part)], all_f.at[f, pl.ds(k * part, part)], sems.at[f * CHUNKS + k]
        )
        for k in range(CHUNKS)
        for f, ref in enumerate((c, d, s, cap, m, v))
    ]
    for copy in copies:
        copy.start()
    for copy in copies:
        copy.wait()
    for out, hi in ((bx0, xeven), (bx1, jnp.logical_not(xeven))):
        one = jnp.where(hi, n - 1, 0)
        two = jnp.where(hi, n - 2, 1)
        for slot, (f, at) in enumerate(
            [(f, i) for f in range(4) for i in (one, two)] + [(4, one), (5, one)]
        ):
            out[slot] = all_f[f, at]

    def tiles(four, low):
        out = None
        for f, value in enumerate(four):
            part = rolled(value, 2 * f if low else 2 * f + 2, 0)
            out = part if f == 0 else jnp.where(row < 2 * f, out, part)
        return out

    def put(at, lo, hi):
        by0[at] = jnp.where(yeven, hi, lo)
        by1[at] = jnp.where(yeven, lo, hi)

    def group(g, _):
        lo = hi = None
        for k in range(8):
            x = g * 4 + k // 2
            if k % 2 == 0:
                put(
                    x,
                    tiles([all_f[f, x, 0:8, :] for f in range(4)], True),
                    tiles([all_f[f, x, 8:16, :] for f in range(4)], False),
                )
            a = rolled(all_f[4 + k % 2, x, 0:8, :], k, 0)
            b = rolled(all_f[4 + k % 2, x, 8:16, :], k + 1, 0)
            lo = a if k == 0 else jnp.where(row < k, lo, a)
            hi = b if k == 0 else jnp.where(row < k, hi, b)
        put(n + g, lo, hi)
        return 0

    lax.fori_loop(0, n // 4, group, 0, unroll=2)
    lane = lanes((8, 128))
    for ys in (ys0, ys1):
        ys[0:4] = jnp.zeros((4, 8, 128), F32)
    for ys, by in ((ys0, by0), (ys1, by1)):
        ys[4] = by[0]
        ys[5] = by[n - 1]

    def ends_of(g, _):
        out = [None] * 4
        for k in range(8):
            x = g * 8 + k
            parts = (by0[x], by1[x], all_f[5, x, 0:8, :], all_f[5, x, 8:16, :])
            for i, value in enumerate(parts):
                part = rolled(value, 4 * k + 2, 1)
                out[i] = part if k == 0 else jnp.where(lane < 4 * k, out[i], part)
        at = g * 32 + 8
        for col in range(2):
            shift = (at - 128 * col) & 127
            here = (lane + 128 * col >= at) & (lane + 128 * col < at + 32)
            one, two, low, high = (pltpu.roll(q, shift, 1) for q in out)
            v0 = jnp.where(yeven, high, low)
            v1 = jnp.where(yeven, low, high)
            for ys, i, value in ((ys0, 0, one), (ys1, 0, two), (ys0, 2, v0), (ys1, 2, v1)):
                ys[i + col] = jnp.where(here, value, ys[i + col])
        return 0

    lax.fori_loop(0, n // 8, ends_of, 0, unroll=2)


def pack_t(all_f, t):
    n = all_f.shape[1]
    lane = lanes((16, 128))
    t[...] = jnp.zeros(t.shape, F32)

    def pack(g, _):
        at = g * 32 + 8
        for f in range(6):
            out = None
            for k in range(8):
                part = rolled(all_f[f, g * 8 + k], 4 * k + 2, 1)
                out = part if k == 0 else jnp.where(lane < 4 * k, out, part)
            out = pltpu.roll(out, at & 127, 1)
            for col in range(2):
                here = (lane + 128 * col >= at) & (lane + 128 * col < at + 32)
                t[f, col] = jnp.where(here, out, t[f, col])
        return 0

    lax.fori_loop(0, n // 8, pack, 0)


def third(hi, lo, f):
    row = rows((8, 128))
    return jnp.where(row < 4, rolled(hi, -2 * f, 0), rolled(lo, 6 - 2 * f, 0))


def pack_b(ends, planes, idx, tm, rx0, rx1, ys0, ys1, t, b0, b1, e0, e1):
    xeven = is_even(idx, 0)
    zeven = is_even(idx, 2)
    left = lanes((24, 128)) % 4 < 2
    row = rows((8, 128))
    lane = lanes((16, 128))
    tiles = [picked(ends, idx, 1, ys0[k], ys1[k]) for k in range(6)]
    for f in range(6):
        halo = picked(ends, idx, 0, rx0[2 * f if f < 4 else 4 + f], rx1[2 * f if f < 4 else 4 + f])
        for col in range(2):
            at = (1, planes + 2)[col]
            part = rolled(halo[col], 4 * at + 2, 1)
            t[f, col, 0:16, :] = jnp.where(lane // 4 == at % 32, part, tm[f, col])
            if f < 4:
                t[f, col, 16:24, :] = third(tiles[col][1], tiles[col][0], f)
            elif f == 4:
                t[f, col, 16:24, :] = jnp.zeros((8, 128), F32)
            else:
                t[f, col, 16:24, :] = jnp.where(row < 4, tiles[2 + col][1], tiles[2 + col][0])
        one, two = (t[f, 0], t[f, 1])
        hi = jnp.where(left, one, pltpu.roll(two, 2, 1))
        lo = jnp.where(left, pltpu.roll(one, 126, 1), two)
        b0[f] = jnp.where(zeven, hi, lo)
        b1[f] = jnp.where(zeven, lo, hi)
    for f in range(4):
        lo, hi = (third(tiles[k][1], tiles[k][0], f) for k in (4, 5))
        e0[f] = jnp.where(xeven, hi, lo)
        e1[f] = jnp.where(xeven, lo, hi)


def pack_c(ends, idx, all_f, rx0, rx1, ry0, ry1, p, a_out):
    n = all_f.shape[1]
    row = rows((8, 128))
    zero = jnp.zeros((8, 128), F32)

    def both(at):
        return picked(ends, idx, 1, ry0[at], ry1[at])

    def group(g, _):
        mvlo, mvhi = both(n + g)
        for k in range(4):
            x = g * 4 + k
            lo, hi = both(x)
            for f in range(6):
                p[f, x + 2, 0:16, :] = all_f[f, x]
                if f < 4:
                    p[f, x + 2, 16:24, :] = third(hi, lo, f)
                else:
                    r = 2 * k + f - 4
                    a, b = (rolled(mvhi, -r, 0), rolled(mvlo, 7 - r, 0))
                    p[f, x + 2, 16:24, :] = jnp.where(row < 4, a, b)
        return 0

    lax.fori_loop(0, n // 4, group, 0)
    for f in range(6):
        slot = 2 * f if f < 4 else 4 + f
        p[f, 1, 0:16, :], p[f, n + 2, 0:16, :] = picked(ends, idx, 0, rx0[slot], rx1[slot])
        if f < 4:
            p[f, 0, 0:16, :], p[f, n + 3, 0:16, :] = picked(ends, idx, 0, rx0[slot + 1], rx1[slot + 1])
        else:
            p[f, 0, 0:16, :] = jnp.zeros((16, 128), F32)
            p[f, n + 3, 0:16, :] = jnp.zeros((16, 128), F32)
        for e in (0, 1, n + 2, n + 3):
            p[f, e, 16:24, :] = zero

    def make(e, _):
        a_out[e] = inverse(p[3, e])
        return 0

    lax.fori_loop(0, n + 4, make, 0, unroll=4)


def wide(ref):
    return jnp.concatenate([ref[0], ref[1]], axis=1)


def ends_up(own, halo, slot):
    return jnp.where(slot == 1, up(own, 1), up(halo, 1))


def ends_down(own, halo, slot):
    return jnp.where(slot == 2, down(own, 1), down(halo, 1))


def ends_flow(k, f):
    kc, ku, kd = k
    fc, fu, fd = f
    fx = (kc + rolled(kc, -4, 1)) * (rolled(fc, -4, 1) - fc)
    fy = (kc + up(kc, 0)) * (up(fc, 0) - fc)
    flux = (fx - rolled(fx, 4, 1)) + (fy - down(fy, 0))
    return flux + ((kc + ku) * (fu - fc) - (kc + kd) * (fc - fd))


def to_ends(store, at, value, slot):
    value = jnp.where(slot == 1, up(value, 1), down(value, 1))
    store[at, 0] = value[:, 0:128]
    store[at, 1] = value[:, 128:256]


def edge(store, at, e, height=24):
    return pltpu.roll(store[at, e >> 5, 0:height, :], (126 - 4 * (e & 31)) & 127, 1)


def back(value, first, lane):
    return jnp.where(lane == 0, first, down(value, 1))


def inverse(cap):
    return DT * jnp.where(cap > 0, 1.0 / jnp.where(cap > 0, cap, 1.0), 0.0)


def forward(
    ends, idx, cw, p_in, a_in, t, rz0, rz1, re0, re1, mask, cls,
    p, v_out, h, a_out, later, later_z, r1, r2, tang, q_s, m, cs,
):
    n = r2.shape[0]
    for f in range(4):
        p[f, 1, 16:24, :], p[f, n + 2, 16:24, :] = picked(ends, idx, 0, re0[f], re1[f])
    for e in (1, n + 2):
        a_out[e, 16:24, :] = inverse(p[3, e, 16:24, :])

    slot = lanes((24, 256)) % 4
    own, halo = ([], [])
    for f in range(6):
        lo, hi = picked(ends, idx, 2, rz0[f], rz1[f])
        h[f, 0] = jnp.where(slot[:, 0:128] < 2, lo, pltpu.roll(hi, 2, 1))
        h[f, 1] = jnp.where(slot[:, 0:128] < 2, pltpu.roll(lo, 126, 1), hi)
        own.append(wide(t.at[f]))
        halo.append(wide(h.at[f]))
    near = [
        (halo[f], ends_up(own[f], halo[f], slot), ends_down(own[f], halo[f], slot)) for f in (0, 1, 2)
    ]
    vel, vel_down = (halo[5], ends_down(own[5], halo[5], slot))
    az = inverse(halo[3])
    qz = (1 / DT) * az * halo[4]
    rate = 0.5 * ends_flow(near[1], near[0]) + (vel_down * near[0][2] - vel * near[0][0])
    lz = near[0][0] + az * rate
    tz = az * (0.5 * ends_flow(near[2], near[0]) - qz * rate)
    later_z[0] = lz[:, 0:128]
    later_z[1] = lz[:, 128:256]
    for at, value in enumerate((halo[0], halo[1], halo[2], halo[5], lz, tz)):
        to_ends(m, at, value, slot)

    lane = lanes((24, 128))

    def first(t, carry):
        c0, d0, s0, fd, fs = carry
        e = t + 1
        c1, d1, s1 = (p[0, e + 1], p[1, e + 1], p[2, e + 1])
        ch, dh, sh, vh = (edge(m, k, e) for k in range(4))
        gx = c1 - c0
        fdx = (d0 + d1) * gx
        fsx = (s0 + s1) * gx
        gy = up(c0, 0) - c0
        fdy = (d0 + up(d0, 0)) * gy
        fsy = (s0 + up(s0, 0)) * gy
        gz = jnp.where(lane == 127, ch, up(c0, 1)) - c0
        fdz = (d0 + jnp.where(lane == 127, dh, up(d0, 1))) * gz
        fsz = (s0 + jnp.where(lane == 127, sh, up(s0, 1))) * gz
        gl = c0 - ch
        vc = p[5, e] * c0
        rate = (fdx - fd) + (fdy - down(fdy, 0)) + (fdz - back(fdz, (d0 + dh) * gl, lane))
        rate = 0.5 * rate + (back(vc, vh * ch, lane) - vc)
        other = (fsx - fs) + (fsy - down(fsy, 0)) + (fsz - back(fsz, (s0 + sh) * gl, lane))
        a = a_out[e]
        q = (1 / DT) * a * p[4, e]
        later[t] = c0 + a * rate
        tang[t] = a * (0.5 * other - q * rate)
        q_s[t] = q[0:16]
        r1[t] = rate[0:16]
        return c1, d1, s1, fdx, fsx

    c0, d0, s0 = (p[0, 0], p[1, 0], p[2, 0])
    c1, d1, s1 = (p[0, 1], p[1, 1], p[2, 1])
    start = (c1, d1, s1, (d0 + d1) * (c1 - c0), (s0 + s1) * (c1 - c0))
    lax.fori_loop(0, n + 2, first, start, unroll=U1)
    lane = lane[0:16]

    def second(x, carry):
        f1, f2, acc = carry
        t = x + 1
        e = t + 1
        l3, t3, d3, s3 = (later[t], tang[t], p[1, e], p[2, e])
        l0, t0, d0, s0 = (q[0:16] for q in (l3, t3, d3, s3))
        gl = later[t + 1, 0:16, :] - l0
        gt = tang[t + 1, 0:16, :] - t0
        dd = d0 + p[1, e + 1, 0:16, :]
        ss = s0 + p[2, e + 1, 0:16, :]
        fl = dd * gl
        ft = dd * gt + ss * gl
        dd = d3 + up(d3, 0)
        gly = up(l3, 0) - l3
        fly = dd * gly
        fty = dd * (up(t3, 0) - t3) + (s3 + up(s3, 0)) * gly
        dh, sh, vh, lh, th = (edge(m, k, e, 16) for k in (1, 2, 3, 4, 5))
        gl = jnp.where(lane == 127, lh, up(l0, 1)) - l0
        gt = jnp.where(lane == 127, th, up(t0, 1)) - t0
        dd = d0 + jnp.where(lane == 127, dh, up(d0, 1))
        ss = s0 + jnp.where(lane == 127, sh, up(s0, 1))
        flz = dd * gl
        ftz = dd * gt + ss * gl
        dd = d0 + dh
        gl = l0 - lh
        flb = back(flz, dd * gl, lane)
        ftb = back(ftz, dd * (t0 - th) + (s0 + sh) * gl, lane)
        vel = p[5, e, 0:16, :]
        vl = vel * l0
        vt = vel * t0
        rate = (fl - f1) + (fly - down(fly, 0))[0:16] + (flz - flb)
        rate = 0.5 * rate + (back(vl, vh * lh, lane) - vl)
        other = (ft - f2) + (fty - down(fty, 0))[0:16] + (ftz - ftb)
        other = 0.5 * other + (back(vt, vh * th, lane) - vt)
        final = t0 + a_out[e, 0:16, :] * (other - q_s[t] * rate)
        r2[x] = rate
        acc = jnp.where(x & 7 == 0, 0.0, acc) + final
        cs[x >> 3] = acc
        return fl, ft, acc

    gl = later[1, 0:16, :] - later[0, 0:16, :]
    gt = tang[1, 0:16, :] - tang[0, 0:16, :]
    dd = p[1, 1, 0:16, :] + p[1, 2, 0:16, :]
    ss = p[2, 1, 0:16, :] + p[2, 2, 0:16, :]
    lax.fori_loop(0, n, second, (dd * gl, dd * gt + ss * gl, jnp.zeros((16, 128), F32)), unroll=U2)

    lane8 = lanes((8, 128))
    row8 = rows((8, 128))
    expand = (
        lanes((16, 128)) // 8 == rows((16, 128))
    ).astype(F32)
    for yv in range(2):
        out = jnp.zeros((8, 128), F32)
        for X in range(n // 8):
            q = cs[X, 8 * yv : 8 * yv + 8, :]
            for k in (1, 2, 4):
                q = q + pltpu.roll(q, k, 0)
            for k in (1, 2, 4):
                q = q + jnp.where(lane8 & k == 0, pltpu.roll(q, 128 - k, 1), pltpu.roll(q, k, 1))
            out = jnp.where(row8 == X + 1, q, out)
        kind = cls[yv]
        weight = jnp.zeros(kind.shape, F32)
        for k in range(cw.shape[0]):
            weight = jnp.where(kind == k, cw[k], weight)
        weight = weight * mask[yv].astype(F32)
        spread = jnp.dot(weight, expand, precision=lax.Precision.HIGHEST, preferred_element_type=F32)
        v_out[yv] = out * spread * (1.0 / 512.0)


def merge(ends, idx, own, rx0, rx1, ry0, ry1, out, edge):
    row = rows((8, 128))
    for yv in range(2):
        lo, hi = picked(ends, idx, 0, rx0[yv], rx1[yv])
        value = jnp.where(row == 0, pltpu.roll(lo, 2, 0), own[yv])
        out[yv + 1] = jnp.where(row == 7, pltpu.roll(hi, 6, 0), value)
    lo = picked(ends, idx, 1, ry0[1], ry1[1])[0]
    hi = picked(ends, idx, 1, ry0[0], ry1[0])[1]
    for k, value in ((0, lo), (1, hi)):
        out[3 * k] = value
        edge[k] = value


def stacked(parts):
    wide_parts = [jnp.broadcast_to(q, (8, 128)) for q in parts]
    last = jnp.where(rows((8, 128)) < 4, wide_parts[3], wide_parts[0])
    return jnp.concatenate([wide_parts[1], wide_parts[2], last], axis=0)


def inner_flow(d0, m0, lane):
    fy = (d0 + up(d0, 0)) * (up(m0, 0) - m0)
    gz = jnp.where(lane == 127, 0.0, up(m0, 1) - m0)
    fz = (d0 + up(d0, 1)) * gz
    return (fy - down(fy, 0)) + (fz - down(fz, 1)), gz


def middle(vox, p, a_in, sc, sf, src):
    n = sf.shape[0] - 2
    for X in range(n // 8 + 2):
        src[X] = stacked([vox[yv, X : X + 1, :] for yv in range(4)])

    def scale(e, _):
        sc[e] = a_in[e] * src[(e + 6) >> 3]
        return 0

    lax.fori_loop(0, n + 4, scale, 0, unroll=4)
    lane = lanes((24, 128))

    def third(t, f0):
        e = t + 1
        m0, d0 = (sc[e], p[1, e])
        fx = (d0 + p[1, e + 1]) * (sc[e + 1] - m0)
        flow, gz = inner_flow(d0, m0, lane)
        sf[t] = a_in[e] * (src[(e + 6) >> 3] + 0.5 * ((fx - f0) + flow) + p[5, e] * gz)
        return fx

    lax.fori_loop(1, n + 1, third, (p[1, 1] + p[1, 2]) * (sc[2] - sc[1]), unroll=U3)


def adjoint(
    ends, idx, vox, rz0, rz1, re0, re1, p, t, h, a_in, later, later_z, r1, r2, sc_in, sf_in,
    gd_out, gc_out, sc, sf, gd, gc, m, sems,
):
    n = r2.shape[0]
    last = n // 8 + 1
    row = rows((8, 128))
    lane = lanes((24, 128))
    plane = {}
    for X in (0, last):
        at = last - 1 if X == 0 else 1
        parts = [vox[yv, X : X + 1, :] for yv in range(4)]
        for k in range(2):
            parts[3 * k] = picked(ends, idx, 0, re0[k, at : at + 1, :], re1[k, at : at + 1, :])[X > 0]
        plane[X] = stacked(parts)
    for X in (1, last - 1):
        plane[X] = stacked([vox[yv, X : X + 1, :] for yv in range(4)])
    for e in (0, 1, n + 2, n + 3):
        sc[e] = a_in[e] * plane[(e + 6) // 8]
    for e in (1, 2, n + 1, n + 2):
        m0, d0 = (sc[e], p[1, e])
        flow, gz = inner_flow(d0, m0, lane)
        flow = flow + (d0 + p[1, e + 1]) * (sc[e + 1] - m0) - (d0 + p[1, e - 1]) * (m0 - sc[e - 1])
        sf[e - 1] = a_in[e] * (plane[(e + 6) // 8] + 0.5 * flow + p[5, e] * gz)

    slot8 = lanes((8, 128)) % 4
    sources = []
    for halo in (False, True):
        cols = []
        for col in range(2):
            here = (lanes((8, 128)) // 4 + 32 * col + 6) // 8 == row
            parts = []
            for yv in range(4):
                lo, hi = picked(ends, idx, 2, rz0[yv], rz1[yv]) if halo else (vox[yv], vox[yv])
                lo = jnp.broadcast_to(lo[:, 127:128], (8, 128))
                hi = jnp.broadcast_to(hi[:, 0:1], (8, 128))
                both = jnp.where(here, jnp.where(slot8 < 2, lo, hi), 0.0)
                for k in (1, 2, 4):
                    both = both + pltpu.roll(both, k, 0)
                parts.append(both)
            cols.append(stacked(parts))
        sources.append(jnp.concatenate(cols, axis=1))

    slot = lanes((24, 256)) % 4
    at, ah = (inverse(wide(t.at[3])), inverse(wide(h.at[3])))
    st, sh = (at * sources[0], ah * sources[1])
    dt, dh = (wide(t.at[1]), wide(h.at[1]))
    su = ends_up(st, sh, slot)
    flow = ends_flow(
        (dh, ends_up(dt, dh, slot), ends_down(dt, dh, slot)), (sh, su, ends_down(st, sh, slot))
    )
    fz = ah * (sources[1] + 0.5 * flow + wide(h.at[5]) * (su - sh))
    for k, value in enumerate((wide(h.at[0]), sh, fz, wide(later_z))):
        to_ends(m, k, value, slot)
    step = jnp.where(slot == 1, up(sh, 1), down(sh, 1)) - st
    both = dt + jnp.where(slot == 1, up(dh, 1), down(dh, 1))
    add = at * step * (0.5 * both + jnp.where(slot == 1, wide(t.at[5]), 0.0))
    m[4, 0] = add[:, 0:128]
    m[4, 1] = add[:, 128:256]
    outer = (lane == 0) | (lane == 127)

    def correct(t, _):
        sf[t] = sf[t] + jnp.where(outer, edge(m, 4, t + 1), 0.0)
        return 0

    lax.fori_loop(0, n + 2, correct, 0, unroll=10)
    lane = lane[0:16]

    def fourth(x, e0):
        t = x + 1
        e = t + 1
        full = (sc[e], later[t], sf[t], p[0, e])
        m0, l0, s0, c0 = (q[0:16] for q in full)
        ex = (m0 - sc[e + 1, 0:16, :]) * (later[t + 1, 0:16, :] - l0)
        ex = ex + (s0 - sf[t + 1, 0:16, :]) * (p[0, e + 1, 0:16, :] - c0)
        m3, l3, s3, c3 = full
        ey = (m3 - up(m3, 0)) * (up(l3, 0) - l3) + (s3 - up(s3, 0)) * (up(c3, 0) - c3)
        ch, mh, sh, lh = (edge(m, k, e, 16) for k in range(4))
        mu, lu, su, cu = (
            jnp.where(lane == 127, b, up(a, 1)) for a, b in ((m0, mh), (l0, lh), (s0, sh), (c0, ch))
        )
        ez = (m0 - mu) * (lu - l0) + (s0 - su) * (cu - c0)
        eb = back(ez, (mh - m0) * (l0 - lh) + (sh - s0) * (c0 - ch), lane)
        gd[x] = 0.5 * ((ex + e0) + (ey + down(ey, 0))[0:16] + (ez + eb))
        gc[x] = (-1 / DT) * a_in[e, 0:16, :] * (m0 * r2[x] + s0 * r1[t])
        return ex

    ex = (sc[1, 0:16, :] - sc[2, 0:16, :]) * (later[1, 0:16, :] - later[0, 0:16, :])
    ex = ex + (sf[0, 0:16, :] - sf[1, 0:16, :]) * (p[0, 2, 0:16, :] - p[0, 1, 0:16, :])
    part = n // 3
    copies = []
    for k in range(3):
        ex = lax.fori_loop(k * part, (k + 1) * part, fourth, ex, unroll=U4)
        for value, out in ((gd, gd_out), (gc, gc_out)):
            here = pl.ds(k * part, part)
            copies.append(pltpu.make_async_copy(value.at[here], out.at[here], sems.at[len(copies)]))
            copies[-1].start()
    for copy in copies:
        copy.wait()


def coarse(x):
    x = jnp.transpose(x, (1, 0, 2))
    return jnp.pad(x, ((0, 0), (1, 1), (0, 0)))


def shards(c, d, s, cap, m, v, mask, cls, cw):
    n = c.shape[0]
    ends = [lax.axis_size(a) - 1 for a in ("gx", "gy", "gz")]
    idx = jnp.stack([lax.axis_index(a) for a in ("gx", "gy", "gz")]).astype(jnp.int32)
    fields = [pltpu.with_memory_space_constraint(f, pltpu.HBM) for f in (c, d, s, cap, m, v)]
    all_f, bx0, bx1, by0, by1, ys0, ys1 = call(
        pack_a,
        [(6, n, 16, 128)] + [(10, 16, 128)] * 2 + [(n + n // 4, 8, 128)] * 2 + [(6, 8, 128)] * 2,
        [SM] + [HB] * 6,
        (idx, *fields),
        [pltpu.SemaphoreType.DMA((6 * CHUNKS,))],
    )
    ys1 = swap(ys1, "gy", 1, "small_y1")
    ys0 = swap(ys0, "gy", 0, "small_y0")
    ry1 = swap(by1, "gy", 1, "large_y1")
    ry0 = swap(by0, "gy", 0, "large_y0")
    rx0 = swap(bx0, "gx", 0, "face_x0")
    rx1 = swap(bx1, "gx", 1, "face_x1")
    (tm,) = call(pack_t, [(6, 2, 16, 128)], [VM], (all_f,))
    t, bz0, bz1, e0, e1 = call(
        partial(pack_b, ends, n),
        [(6, 2, 24, 128), (6, 24, 128), (6, 24, 128), (4, 8, 128), (4, 8, 128)],
        [SM] + [VM] * 5,
        (idx, tm, rx0, rx1, ys0, ys1),
    )
    p, a = call(
        partial(pack_c, ends),
        [(6, n + 4, 24, 128), (n + 4, 24, 128)],
        [SM] + [VM] * 5,
        (idx, all_f, rx0, rx1, ry0, ry1),
    )
    rz1 = swap(bz1, "gz", 1, "ends_z1")
    rz0 = swap(bz0, "gz", 0, "ends_z0")
    re0 = swap(e0, "gx", 0, "rows_x0")
    re1 = swap(e1, "gx", 1, "rows_x1")
    p, vox, h, a, later, later_z, r1, r2 = call(
        partial(forward, ends),
        [
            (6, n + 4, 24, 128),
            (2, 8, 128),
            (6, 2, 24, 128),
            (n + 4, 24, 128),
            (n + 2, 24, 128),
            (2, 24, 128),
            (n + 2, 16, 128),
            (n, 16, 128),
        ],
        [SM, SM] + [VM] * 9,
        (idx, cw, p, a, t, rz0, rz1, re0, re1, coarse(mask), coarse(cls)),
        [
            pltpu.VMEM((n + 2, 24, 128), F32),
            pltpu.VMEM((n + 2, 16, 128), F32),
            pltpu.VMEM((6, 2, 24, 128), F32),
            pltpu.VMEM((n // 8, 16, 128), F32),
        ],
        alias={2: 0, 3: 3},
    )
    ry1 = swap(vox, "gy", 1, "voxel_y1")
    ry0 = swap(vox, "gy", 0, "voxel_y0")
    rx0 = swap(vox, "gx", 0, "voxel_x0")
    rx1 = swap(vox, "gx", 1, "voxel_x1")
    vox, edge = call(
        partial(merge, ends), [(4, 8, 128), (2, 8, 128)], [SM] + [VM] * 5, (idx, vox, rx0, rx1, ry0, ry1), limit=1
    )
    rz1 = swap(vox, "gz", 1, "voxel_z1")
    rz0 = swap(vox, "gz", 0, "voxel_z0")
    re0 = swap(edge, "gx", 0, "corner_x0")
    re1 = swap(edge, "gx", 1, "corner_x1")
    sc, sf = call(
        middle,
        [(n + 4, 24, 128), (n + 2, 24, 128)],
        [VM] * 3,
        (vox, p, a),
        [pltpu.VMEM((n // 8 + 2, 24, 128), F32)],
    )
    gd, gc, _, _ = call(
        partial(adjoint, ends),
        [(n, 16, 128)] * 2 + [(n + 4, 24, 128), (n + 2, 24, 128)],
        [SM] + [VM] * 15,
        (idx, vox, rz0, rz1, re0, re1, p, t, h, a, later, later_z, r1, r2, sc, sf),
        [
            pltpu.VMEM((n, 16, 128), F32),
            pltpu.VMEM((n, 16, 128), F32),
            pltpu.VMEM((5, 2, 24, 128), F32),
            pltpu.SemaphoreType.DMA((6,)),
        ],
        alias={14: 2, 15: 3},
        hbm=2,
    )
    return gd, gc


def solution(mesh):
    spec = P("gx", "gy", "gz")
    return jax.shard_map(
        shards, mesh=mesh, in_specs=(spec,) * 8 + (P(),), out_specs=(spec, spec), check_vma=False
    )
```

```python
from functools import partial

import jax
import jax.numpy as jnp
from jax import lax
from jax.experimental import pallas as pl
from jax.experimental.pallas import tpu as pltpu
from jax.sharding import PartitionSpec as P


DT = 0.1
CHUNKS = 1
U1, U2, U3, U4 = (5, 4, 8, 8)
F32 = jnp.float32
VM = pl.BlockSpec(memory_space=pltpu.VMEM)
SM = pl.BlockSpec(memory_space=pltpu.SMEM)
HB = pl.BlockSpec(memory_space=pltpu.HBM)


def swap_pairs(size, first, ends=True):
    pairs = []
    for i in range(first, size if ends else size - 1, 2):
        pairs += [(i, (i + 1) % size), ((i + 1) % size, i)]
    return pairs


def swap(value, axis, first, name):
    ends = name not in PARTIAL
    return lax.ppermute(value, axis, swap_pairs(lax.axis_size(axis), first, ends))


PARTIAL = ()


def call(body, outs, specs, args, scratch=(), limit=24, alias=None, hbm=0):
    return pl.pallas_call(
        body,
        out_shape=[jax.ShapeDtypeStruct(s, F32) for s in outs],
        in_specs=specs,
        out_specs=[HB] * hbm + [VM] * (len(outs) - hbm),
        scratch_shapes=list(scratch),
        input_output_aliases=alias or {},
        compiler_params=pltpu.CompilerParams(vmem_limit_bytes=limit << 20),
    )(*args)


def rows(shape):
    return lax.broadcasted_iota(jnp.int32, shape, len(shape) - 2)


def lanes(shape):
    return lax.broadcasted_iota(jnp.int32, shape, len(shape) - 1)


def up(x, axis):
    return pltpu.roll(x, x.shape[axis] - 1, axis)


def down(x, axis):
    return pltpu.roll(x, 1, axis)


def rolled(x, shift, axis):
    shift = shift % x.shape[axis]
    return x if shift == 0 else pltpu.roll(x, shift, axis)


def is_even(idx, axis):
    return idx[axis] % 2 == 0


def picked(ends, idx, axis, r0, r1):
    even = is_even(idx, axis)
    lo = jnp.where(even, r1, r0)
    hi = jnp.where(even, r0, r1)
    return jnp.where(idx[axis] > 0, lo, 0.0), jnp.where(idx[axis] < ends[axis], hi, 0.0)


def pack_a(idx, c, d, s, cap, m, v, all_f, bx0, bx1, by0, by1, ys0, ys1, second, sems):
    n = c.shape[0]
    xeven = is_even(idx, 0)
    yeven = is_even(idx, 1)
    row = rows((8, 128))
    part = n // CHUNKS
    copies = [
        pltpu.make_async_copy(
            ref.at[pl.ds(k * part, part)], all_f.at[f, pl.ds(k * part, part)], sems.at[f * CHUNKS + k]
        )
        for k in range(CHUNKS)
        for f, ref in enumerate((c, d, s, cap, m, v))
    ]
    for copy in copies:
        copy.start()
    for copy in copies:
        copy.wait()
    for out, hi in ((bx0, xeven), (bx1, jnp.logical_not(xeven))):
        one = jnp.where(hi, n - 1, 0)
        two = jnp.where(hi, n - 2, 1)
        for slot, (f, at) in enumerate(
            [(f, i) for f in range(4) for i in (one, two)] + [(4, one), (5, one)]
        ):
            out[slot] = all_f[f, at]

    def tiles(five, low):
        out = None
        for f, value in enumerate(five[:4]):
            part = rolled(value, 2 * f if low else 2 * f + 2, 0)
            out = part if f == 0 else jnp.where(row < 2 * f, out, part)
        if low:
            return jnp.where(row == 7, rolled(five[4], 7, 0), out)
        return jnp.where(row == 6, rolled(five[4], 7, 0), out)

    def put(at, lo, hi):
        by0[at] = jnp.where(yeven, hi, lo)
        by1[at] = jnp.where(yeven, lo, hi)

    def group(g, _):
        lo = hi = clo = chi = None
        for k in range(8):
            x = g * 8 + k
            low = [all_f[f, x, 0:8, :] for f in range(6)]
            high = [all_f[f, x, 8:16, :] for f in range(6)]
            put(x, tiles(low, True), tiles(high, False))
            a, b = (rolled(low[5], k, 0), rolled(high[5], k + 1, 0))
            lo = a if k == 0 else jnp.where(row < k, lo, a)
            hi = b if k == 0 else jnp.where(row < k, hi, b)
            a, b = (rolled(low[3], k - 1, 0), rolled(high[3], k + 2, 0))
            clo = a if k == 0 else jnp.where(row < k, clo, a)
            chi = b if k == 0 else jnp.where(row < k, chi, b)
        put(n + g, lo, hi)
        second[0, g] = clo
        second[1, g] = chi
        return 0

    lax.fori_loop(0, n // 8, group, 0)
    lane = lanes((8, 128))
    for ys in (ys0, ys1):
        ys[0:4] = jnp.zeros((4, 8, 128), F32)
    for ys, by in ((ys0, by0), (ys1, by1)):
        ys[4] = by[0]
        ys[5] = by[n - 1]

    def ends_of(g, _):
        out = [None] * 4
        for k in range(8):
            x = g * 8 + k
            parts = (by0[x], by1[x], all_f[5, x, 0:8, :], all_f[5, x, 8:16, :])
            for i, value in enumerate(parts):
                part = rolled(value, 4 * k + 2, 1)
                out[i] = part if k == 0 else jnp.where(lane < 4 * k, out[i], part)
        at = g * 32 + 8
        for col in range(2):
            shift = (at - 128 * col) & 127
            here = (lane + 128 * col >= at) & (lane + 128 * col < at + 32)
            one, two, low, high = (pltpu.roll(q, shift, 1) for q in out)
            v0 = jnp.where(yeven, high, low)
            v1 = jnp.where(yeven, low, high)
            for ys, i, value in ((ys0, 0, one), (ys1, 0, two), (ys0, 2, v0), (ys1, 2, v1)):
                ys[i + col] = jnp.where(here, value, ys[i + col])
        return 0

    lax.fori_loop(0, n // 8, ends_of, 0, unroll=2)


def pack_t(all_f, t):
    n = all_f.shape[1]
    lane = lanes((16, 128))
    t[...] = jnp.zeros(t.shape, F32)

    def pack(g, _):
        at = g * 32 + 8
        for f in range(6):
            out = None
            for k in range(8):
                part = rolled(all_f[f, g * 8 + k], 4 * k + 2, 1)
                out = part if k == 0 else jnp.where(lane < 4 * k, out, part)
            out = pltpu.roll(out, at & 127, 1)
            for col in range(2):
                here = (lane + 128 * col >= at) & (lane + 128 * col < at + 32)
                t[f, col] = jnp.where(here, out, t[f, col])
        return 0

    lax.fori_loop(0, n // 8, pack, 0)


def third(hi, lo, f):
    row = rows((8, 128))
    return jnp.where(row < 4, rolled(hi, -2 * f, 0), rolled(lo, 6 - 2 * f, 0))


def pack_b(ends, planes, idx, tm, rx0, rx1, ys0, ys1, t, b0, b1, e0, e1):
    xeven = is_even(idx, 0)
    zeven = is_even(idx, 2)
    left = lanes((24, 128)) % 4 < 2
    row = rows((8, 128))
    lane = lanes((16, 128))
    tiles = [picked(ends, idx, 1, ys0[k], ys1[k]) for k in range(6)]
    for f in range(6):
        halo = picked(ends, idx, 0, rx0[2 * f if f < 4 else 4 + f], rx1[2 * f if f < 4 else 4 + f])
        for col in range(2):
            at = (1, planes + 2)[col]
            part = rolled(halo[col], 4 * at + 2, 1)
            t[f, col, 0:16, :] = jnp.where(lane // 4 == at % 32, part, tm[f, col])
            if f < 4:
                t[f, col, 16:24, :] = third(tiles[col][1], tiles[col][0], f)
            elif f == 4:
                t[f, col, 16:24, :] = jnp.zeros((8, 128), F32)
            else:
                t[f, col, 16:24, :] = jnp.where(row < 4, tiles[2 + col][1], tiles[2 + col][0])
        one, two = (t[f, 0], t[f, 1])
        hi = jnp.where(left, one, pltpu.roll(two, 2, 1))
        lo = jnp.where(left, pltpu.roll(one, 126, 1), two)
        b0[f] = jnp.where(zeven, hi, lo)
        b1[f] = jnp.where(zeven, lo, hi)
    for f in range(4):
        lo, hi = (third(tiles[k][1], tiles[k][0], f) for k in (4, 5))
        e0[f] = jnp.where(xeven, hi, lo)
        e1[f] = jnp.where(xeven, lo, hi)


def pack_main(ends, idx, all_f, rx0, rx1, p, a_out):
    n = all_f.shape[1]

    def plane(x, _):
        for f in range(6):
            p[f, x + 2, 0:16, :] = all_f[f, x]
        a_out[x + 2, 0:16, :] = inverse(all_f[3, x])
        return 0

    lax.fori_loop(0, n, plane, 0, unroll=4)
    zero = jnp.zeros((16, 128), F32)
    for f in range(6):
        slot = 2 * f if f < 4 else 4 + f
        p[f, 1, 0:16, :], p[f, n + 2, 0:16, :] = picked(ends, idx, 0, rx0[slot], rx1[slot])
        p[f, 0, 0:16, :], p[f, n + 3, 0:16, :] = (
            picked(ends, idx, 0, rx0[slot + 1], rx1[slot + 1]) if f < 4 else (zero, zero)
        )
        for e in (0, 1, n + 2, n + 3):
            p[f, e, 16:24, :] = zero[0:8]
    for e in (0, 1, n + 2, n + 3):
        a_out[e, 0:16, :] = inverse(p[3, e, 0:16, :])
        a_out[e, 16:24, :] = zero[0:8]


def pack_c(ends, idx, ry0, ry1, p_in, a_in, p, a_out):
    n = p.shape[1] - 4
    row = rows((8, 128))

    def both(at):
        return picked(ends, idx, 1, ry0[at], ry1[at])

    def group(g, _):
        vlo, vhi = both(n + g)
        for k in range(8):
            x = g * 8 + k
            lo, hi = both(x)
            for f in range(4):
                value = third(hi, lo, f)
                p[f, x + 2, 16:24, :] = value
            a_out[x + 2, 16:24, :] = inverse(value)
            p[4, x + 2, 16:24, :] = jnp.where(row < 4, rolled(hi, 1, 0), rolled(lo, 1, 0))
            p[5, x + 2, 16:24, :] = jnp.where(row < 4, rolled(vhi, -k, 0), rolled(vlo, 7 - k, 0))
        return 0

    lax.fori_loop(0, n // 8, group, 0)


def wide(ref):
    return jnp.concatenate([ref[0], ref[1]], axis=1)


def ends_up(own, halo, slot):
    return jnp.where(slot == 1, up(own, 1), up(halo, 1))


def ends_down(own, halo, slot):
    return jnp.where(slot == 2, down(own, 1), down(halo, 1))


def ends_flow(k, f):
    kc, ku, kd = k
    fc, fu, fd = f
    fx = (kc + rolled(kc, -4, 1)) * (rolled(fc, -4, 1) - fc)
    fy = (kc + up(kc, 0)) * (up(fc, 0) - fc)
    flux = (fx - rolled(fx, 4, 1)) + (fy - down(fy, 0))
    return flux + ((kc + ku) * (fu - fc) - (kc + kd) * (fc - fd))


def to_ends(store, at, value, slot):
    value = jnp.where(slot == 1, up(value, 1), down(value, 1))
    store[at, 0] = value[:, 0:128]
    store[at, 1] = value[:, 128:256]


def edge(store, at, e, height=24):
    return pltpu.roll(store[at, e >> 5, 0:height, :], (126 - 4 * (e & 31)) & 127, 1)


def back(value, first, lane):
    return jnp.where(lane == 0, first, down(value, 1))


def inverse(cap):
    return DT * jnp.where(cap > 0, 1.0 / jnp.where(cap > 0, cap, 1.0), 0.0)


def forward(
    ends, idx, cw, p_in, a_in, t, rz0, rz1, re0, re1, mask, cls, rows2,
    p, v_out, vy0, vy1, h, a_out, later, later_z, r1, r2, tang, q_s, m, cs,
):
    n = r2.shape[0]
    for f in range(4):
        p[f, 1, 16:24, :], p[f, n + 2, 16:24, :] = picked(ends, idx, 0, re0[f], re1[f])
    for e in (1, n + 2):
        a_out[e, 16:24, :] = inverse(p[3, e, 16:24, :])

    slot = lanes((24, 256)) % 4
    own, halo = ([], [])
    for f in range(6):
        lo, hi = picked(ends, idx, 2, rz0[f], rz1[f])
        h[f, 0] = jnp.where(slot[:, 0:128] < 2, lo, pltpu.roll(hi, 2, 1))
        h[f, 1] = jnp.where(slot[:, 0:128] < 2, pltpu.roll(lo, 126, 1), hi)
        own.append(wide(t.at[f]))
        halo.append(wide(h.at[f]))
    near = [
        (halo[f], ends_up(own[f], halo[f], slot), ends_down(own[f], halo[f], slot)) for f in (0, 1, 2)
    ]
    vel, vel_down = (halo[5], ends_down(own[5], halo[5], slot))
    az = inverse(halo[3])
    qz = (1 / DT) * az * halo[4]
    rate = 0.5 * ends_flow(near[1], near[0]) + (vel_down * near[0][2] - vel * near[0][0])
    lz = near[0][0] + az * rate
    tz = az * (0.5 * ends_flow(near[2], near[0]) - qz * rate)
    later_z[0] = lz[:, 0:128]
    later_z[1] = lz[:, 128:256]
    for at, value in enumerate((halo[0], halo[1], halo[2], halo[5], lz, tz)):
        to_ends(m, at, value, slot)

    lane = lanes((24, 128))

    def first(t, carry):
        c0, d0, s0, fd, fs = carry
        e = t + 1
        c1, d1, s1 = (p[0, e + 1], p[1, e + 1], p[2, e + 1])
        ch, dh, sh, vh = (edge(m, k, e) for k in range(4))
        gx = c1 - c0
        fdx = (d0 + d1) * gx
        fsx = (s0 + s1) * gx
        gy = up(c0, 0) - c0
        fdy = (d0 + up(d0, 0)) * gy
        fsy = (s0 + up(s0, 0)) * gy
        gz = jnp.where(lane == 127, ch, up(c0, 1)) - c0
        fdz = (d0 + jnp.where(lane == 127, dh, up(d0, 1))) * gz
        fsz = (s0 + jnp.where(lane == 127, sh, up(s0, 1))) * gz
        gl = c0 - ch
        vc = p[5, e] * c0
        rate = (fdx - fd) + (fdy - down(fdy, 0)) + (fdz - back(fdz, (d0 + dh) * gl, lane))
        rate = 0.5 * rate + (back(vc, vh * ch, lane) - vc)
        other = (fsx - fs) + (fsy - down(fsy, 0)) + (fsz - back(fsz, (s0 + sh) * gl, lane))
        a = a_out[e]
        q = (1 / DT) * a * p[4, e]
        later[t] = c0 + a * rate
        tang[t] = a * (0.5 * other - q * rate)
        q_s[t] = q[0:16]
        r1[t] = rate[0:16]
        return c1, d1, s1, fdx, fsx

    c0, d0, s0 = (p[0, 0], p[1, 0], p[2, 0])
    c1, d1, s1 = (p[0, 1], p[1, 1], p[2, 1])
    start = (c1, d1, s1, (d0 + d1) * (c1 - c0), (s0 + s1) * (c1 - c0))
    lax.fori_loop(0, n + 2, first, start, unroll=U1)
    lane = lane[0:16]

    def second(x, carry):
        f1, f2, acc = carry
        t = x + 1
        e = t + 1
        l3, t3, d3, s3 = (later[t], tang[t], p[1, e], p[2, e])
        l0, t0, d0, s0 = (q[0:16] for q in (l3, t3, d3, s3))
        gl = later[t + 1, 0:16, :] - l0
        gt = tang[t + 1, 0:16, :] - t0
        dd = d0 + p[1, e + 1, 0:16, :]
        ss = s0 + p[2, e + 1, 0:16, :]
        fl = dd * gl
        ft = dd * gt + ss * gl
        dd = d3 + up(d3, 0)
        gly = up(l3, 0) - l3
        fly = dd * gly
        fty = dd * (up(t3, 0) - t3) + (s3 + up(s3, 0)) * gly
        dh, sh, vh, lh, th = (edge(m, k, e, 16) for k in (1, 2, 3, 4, 5))
        gl = jnp.where(lane == 127, lh, up(l0, 1)) - l0
        gt = jnp.where(lane == 127, th, up(t0, 1)) - t0
        dd = d0 + jnp.where(lane == 127, dh, up(d0, 1))
        ss = s0 + jnp.where(lane == 127, sh, up(s0, 1))
        flz = dd * gl
        ftz = dd * gt + ss * gl
        dd = d0 + dh
        gl = l0 - lh
        flb = back(flz, dd * gl, lane)
        ftb = back(ftz, dd * (t0 - th) + (s0 + sh) * gl, lane)
        vel = p[5, e, 0:16, :]
        vl = vel * l0
        vt = vel * t0
        rate = (fl - f1) + (fly - down(fly, 0))[0:16] + (flz - flb)
        rate = 0.5 * rate + (back(vl, vh * lh, lane) - vl)
        other = (ft - f2) + (fty - down(fty, 0))[0:16] + (ftz - ftb)
        other = 0.5 * other + (back(vt, vh * th, lane) - vt)
        final = t0 + a_out[e, 0:16, :] * (other - q_s[t] * rate)
        r2[x] = rate
        acc = jnp.where(x & 7 == 0, 0.0, acc) + final
        cs[x >> 3] = acc
        return fl, ft, acc

    gl = later[1, 0:16, :] - later[0, 0:16, :]
    gt = tang[1, 0:16, :] - tang[0, 0:16, :]
    dd = p[1, 1, 0:16, :] + p[1, 2, 0:16, :]
    ss = p[2, 1, 0:16, :] + p[2, 2, 0:16, :]
    lax.fori_loop(0, n, second, (dd * gl, dd * gt + ss * gl, jnp.zeros((16, 128), F32)), unroll=U2)

    lane8 = lanes((8, 128))
    row8 = rows((8, 128))
    expand = (
        lanes((16, 128)) // 8 == rows((16, 128))
    ).astype(F32)
    for yv in range(2):
        out = jnp.zeros((8, 128), F32)
        for X in range(n // 8):
            q = cs[X, 8 * yv : 8 * yv + 8, :]
            for k in (1, 2, 4):
                q = q + pltpu.roll(q, k, 0)
            for k in (1, 2, 4):
                q = q + jnp.where(lane8 & k == 0, pltpu.roll(q, 128 - k, 1), pltpu.roll(q, k, 1))
            out = jnp.where(row8 == X + 1, q, out)
        kind = cls[yv]
        weight = jnp.zeros(kind.shape, F32)
        for k in range(cw.shape[0]):
            weight = jnp.where(kind == k, cw[k], weight)
        weight = weight * mask[yv].astype(F32)
        spread = jnp.dot(weight, expand, precision=lax.Precision.HIGHEST, preferred_element_type=F32)
        v_out[yv] = out * spread * (1.0 / 512.0)
        vy0[yv] = v_out[yv]
        vy1[yv] = v_out[yv]
    yeven = is_even(idx, 1)
    for g in range(rows2.shape[1]):
        lo, hi = (inverse(rows2[k, g]) for k in range(2))
        vy0[2 + g] = jnp.where(yeven, hi, lo)
        vy1[2 + g] = jnp.where(yeven, lo, hi)


def merge(ends, idx, own, rx0, rx1, ry0, ry1, out, edge, a2):
    row = rows((8, 128))
    for yv in range(2):
        lo, hi = picked(ends, idx, 0, rx0[yv], rx1[yv])
        value = jnp.where(row == 0, pltpu.roll(lo, 2, 0), own[yv])
        out[yv + 1] = jnp.where(row == 7, pltpu.roll(hi, 6, 0), value)
    lo = picked(ends, idx, 1, ry0[1], ry1[1])[0]
    hi = picked(ends, idx, 1, ry0[0], ry1[0])[1]
    for g in range(a2.shape[1]):
        a2[0, g], a2[1, g] = picked(ends, idx, 1, ry0[2 + g], ry1[2 + g])
    for k, value in ((0, lo), (1, hi)):
        out[3 * k] = value
        edge[k] = value


def stacked(parts):
    wide_parts = [jnp.broadcast_to(q, (8, 128)) for q in parts]
    last = jnp.where(rows((8, 128)) < 4, wide_parts[3], wide_parts[0])
    return jnp.concatenate([wide_parts[1], wide_parts[2], last], axis=0)


def inner_flow(d0, m0, lane):
    fy = (d0 + up(d0, 0)) * (up(m0, 0) - m0)
    gz = jnp.where(lane == 127, 0.0, up(m0, 1) - m0)
    fz = (d0 + up(d0, 1)) * gz
    return (fy - down(fy, 0)) + (fz - down(fz, 1)), gz


def middle(vox, p, a_in, a2, sc, sf, src):
    n = sf.shape[0] - 2
    for X in range(n // 8 + 2):
        src[X] = stacked([vox[yv, X : X + 1, :] for yv in range(4)])

    def scale(e, _):
        sc[e] = a_in[e] * src[(e + 6) >> 3]
        return 0

    lax.fori_loop(0, n + 4, scale, 0, unroll=4)
    row = rows((8, 128))

    def second(g, _):
        for k in range(8):
            e = g * 8 + k + 2
            lo, hi = (rolled(a2[0, g], 6 - k, 0), rolled(a2[1, g], 1 - k, 0))
            a3 = a_in[e, 16:24, :]
            a3 = jnp.where(row == 1, hi, jnp.where(row == 6, lo, a3))
            sc[e, 16:24, :] = a3 * src[g + 1, 16:24, :]
        return 0

    lax.fori_loop(0, n // 8, second, 0)
    lane = lanes((24, 128))

    def third(t, f0):
        e = t + 1
        m0, d0 = (sc[e], p[1, e])
        fx = (d0 + p[1, e + 1]) * (sc[e + 1] - m0)
        flow, gz = inner_flow(d0, m0, lane)
        sf[t] = a_in[e] * (src[(e + 6) >> 3] + 0.5 * ((fx - f0) + flow) + p[5, e] * gz)
        return fx

    lax.fori_loop(1, n + 1, third, (p[1, 1] + p[1, 2]) * (sc[2] - sc[1]), unroll=U3)


def adjoint(
    ends, idx, vox, rz0, rz1, re0, re1, p, t, h, a_in, later, later_z, r1, r2, sc_in, sf_in,
    gd_out, gc_out, sc, sf, gd, gc, m, sems,
):
    n = r2.shape[0]
    last = n // 8 + 1
    row = rows((8, 128))
    lane = lanes((24, 128))
    plane = {}
    for X in (0, last):
        at = last - 1 if X == 0 else 1
        parts = [vox[yv, X : X + 1, :] for yv in range(4)]
        for k in range(2):
            parts[3 * k] = picked(ends, idx, 0, re0[k, at : at + 1, :], re1[k, at : at + 1, :])[X > 0]
        plane[X] = stacked(parts)
    for X in (1, last - 1):
        plane[X] = stacked([vox[yv, X : X + 1, :] for yv in range(4)])
    for e in (0, 1, n + 2, n + 3):
        sc[e] = a_in[e] * plane[(e + 6) // 8]
    for e in (1, 2, n + 1, n + 2):
        m0, d0 = (sc[e], p[1, e])
        flow, gz = inner_flow(d0, m0, lane)
        flow = flow + (d0 + p[1, e + 1]) * (sc[e + 1] - m0) - (d0 + p[1, e - 1]) * (m0 - sc[e - 1])
        sf[e - 1] = a_in[e] * (plane[(e + 6) // 8] + 0.5 * flow + p[5, e] * gz)

    slot8 = lanes((8, 128)) % 4
    sources = []
    for halo in (False, True):
        cols = []
        for col in range(2):
            here = (lanes((8, 128)) // 4 + 32 * col + 6) // 8 == row
            parts = []
            for yv in range(4):
                lo, hi = picked(ends, idx, 2, rz0[yv], rz1[yv]) if halo else (vox[yv], vox[yv])
                lo = jnp.broadcast_to(lo[:, 127:128], (8, 128))
                hi = jnp.broadcast_to(hi[:, 0:1], (8, 128))
                both = jnp.where(here, jnp.where(slot8 < 2, lo, hi), 0.0)
                for k in (1, 2, 4):
                    both = both + pltpu.roll(both, k, 0)
                parts.append(both)
            cols.append(stacked(parts))
        sources.append(jnp.concatenate(cols, axis=1))

    slot = lanes((24, 256)) % 4
    at, ah = (inverse(wide(t.at[3])), inverse(wide(h.at[3])))
    st, sh = (at * sources[0], ah * sources[1])
    dt, dh = (wide(t.at[1]), wide(h.at[1]))
    su = ends_up(st, sh, slot)
    flow = ends_flow(
        (dh, ends_up(dt, dh, slot), ends_down(dt, dh, slot)), (sh, su, ends_down(st, sh, slot))
    )
    fz = ah * (sources[1] + 0.5 * flow + wide(h.at[5]) * (su - sh))
    for k, value in enumerate((wide(h.at[0]), sh, fz, wide(later_z))):
        to_ends(m, k, value, slot)
    step = jnp.where(slot == 1, up(sh, 1), down(sh, 1)) - st
    both = dt + jnp.where(slot == 1, up(dh, 1), down(dh, 1))
    add = at * step * (0.5 * both + jnp.where(slot == 1, wide(t.at[5]), 0.0))
    m[4, 0] = add[:, 0:128]
    m[4, 1] = add[:, 128:256]
    outer = (lane == 0) | (lane == 127)

    def correct(t, _):
        sf[t] = sf[t] + jnp.where(outer, edge(m, 4, t + 1), 0.0)
        return 0

    lax.fori_loop(0, n + 2, correct, 0, unroll=10)
    lane = lane[0:16]

    def fourth(x, e0):
        t = x + 1
        e = t + 1
        full = (sc[e], later[t], sf[t], p[0, e])
        m0, l0, s0, c0 = (q[0:16] for q in full)
        ex = (m0 - sc[e + 1, 0:16, :]) * (later[t + 1, 0:16, :] - l0)
        ex = ex + (s0 - sf[t + 1, 0:16, :]) * (p[0, e + 1, 0:16, :] - c0)
        m3, l3, s3, c3 = full
        ey = (m3 - up(m3, 0)) * (up(l3, 0) - l3) + (s3 - up(s3, 0)) * (up(c3, 0) - c3)
        ch, mh, sh, lh = (edge(m, k, e, 16) for k in range(4))
        mu, lu, su, cu = (
            jnp.where(lane == 127, b, up(a, 1)) for a, b in ((m0, mh), (l0, lh), (s0, sh), (c0, ch))
        )
        ez = (m0 - mu) * (lu - l0) + (s0 - su) * (cu - c0)
        eb = back(ez, (mh - m0) * (l0 - lh) + (sh - s0) * (c0 - ch), lane)
        gd[x] = 0.5 * ((ex + e0) + (ey + down(ey, 0))[0:16] + (ez + eb))
        gc[x] = (-1 / DT) * a_in[e, 0:16, :] * (m0 * r2[x] + s0 * r1[t])
        return ex

    ex = (sc[1, 0:16, :] - sc[2, 0:16, :]) * (later[1, 0:16, :] - later[0, 0:16, :])
    ex = ex + (sf[0, 0:16, :] - sf[1, 0:16, :]) * (p[0, 2, 0:16, :] - p[0, 1, 0:16, :])
    part = n // 3
    copies = []
    for k in range(3):
        ex = lax.fori_loop(k * part, (k + 1) * part, fourth, ex, unroll=U4)
        for value, out in ((gd, gd_out), (gc, gc_out)):
            here = pl.ds(k * part, part)
            copies.append(pltpu.make_async_copy(value.at[here], out.at[here], sems.at[len(copies)]))
            copies[-1].start()
    for copy in copies:
        copy.wait()


def coarse(x):
    x = jnp.transpose(x, (1, 0, 2))
    return jnp.pad(x, ((0, 0), (1, 1), (0, 0)))


def shards(c, d, s, cap, m, v, mask, cls, cw):
    n = c.shape[0]
    ends = [lax.axis_size(a) - 1 for a in ("gx", "gy", "gz")]
    idx = jnp.stack([lax.axis_index(a) for a in ("gx", "gy", "gz")]).astype(jnp.int32)
    fields = [pltpu.with_memory_space_constraint(f, pltpu.HBM) for f in (c, d, s, cap, m, v)]
    all_f, bx0, bx1, by0, by1, ys0, ys1, second = call(
        pack_a,
        [(6, n, 16, 128)]
        + [(10, 16, 128)] * 2
        + [(n + n // 8, 8, 128)] * 2
        + [(6, 8, 128)] * 2
        + [(2, n // 8, 8, 128)],
        [SM] + [HB] * 6,
        (idx, *fields),
        [pltpu.SemaphoreType.DMA((6 * CHUNKS,))],
    )
    ys1 = swap(ys1, "gy", 1, "small_y1")
    ys0 = swap(ys0, "gy", 0, "small_y0")
    ry1 = swap(by1, "gy", 1, "large_y1")
    ry0 = swap(by0, "gy", 0, "large_y0")
    rx0 = swap(bx0, "gx", 0, "face_x0")
    rx1 = swap(bx1, "gx", 1, "face_x1")
    (tm,) = call(pack_t, [(6, 2, 16, 128)], [VM], (all_f,))
    t, bz0, bz1, e0, e1 = call(
        partial(pack_b, ends, n),
        [(6, 2, 24, 128), (6, 24, 128), (6, 24, 128), (4, 8, 128), (4, 8, 128)],
        [SM] + [VM] * 5,
        (idx, tm, rx0, rx1, ys0, ys1),
    )
    p, a = call(
        partial(pack_main, ends),
        [(6, n + 4, 24, 128), (n + 4, 24, 128)],
        [SM] + [VM] * 3,
        (idx, all_f, rx0, rx1),
    )
    p, a = call(
        partial(pack_c, ends),
        [(6, n + 4, 24, 128), (n + 4, 24, 128)],
        [SM] + [VM] * 4,
        (idx, ry0, ry1, p, a),
        alias={3: 0, 4: 1},
    )
    rz1 = swap(bz1, "gz", 1, "ends_z1")
    rz0 = swap(bz0, "gz", 0, "ends_z0")
    re0 = swap(e0, "gx", 0, "rows_x0")
    re1 = swap(e1, "gx", 1, "rows_x1")
    p, vox, vy0, vy1, h, a, later, later_z, r1, r2 = call(
        partial(forward, ends),
        [
            (6, n + 4, 24, 128),
            (2, 8, 128),
            (2 + n // 8, 8, 128),
            (2 + n // 8, 8, 128),
            (6, 2, 24, 128),
            (n + 4, 24, 128),
            (n + 2, 24, 128),
            (2, 24, 128),
            (n + 2, 16, 128),
            (n, 16, 128),
        ],
        [SM, SM] + [VM] * 10,
        (idx, cw, p, a, t, rz0, rz1, re0, re1, coarse(mask), coarse(cls), second),
        [
            pltpu.VMEM((n + 2, 24, 128), F32),
            pltpu.VMEM((n + 2, 16, 128), F32),
            pltpu.VMEM((6, 2, 24, 128), F32),
            pltpu.VMEM((n // 8, 16, 128), F32),
        ],
        alias={2: 0, 3: 5},
    )
    ry1 = swap(vy1, "gy", 1, "voxel_y1")
    ry0 = swap(vy0, "gy", 0, "voxel_y0")
    rx0 = swap(vox, "gx", 0, "voxel_x0")
    rx1 = swap(vox, "gx", 1, "voxel_x1")
    vox, edge, a2 = call(
        partial(merge, ends),
        [(4, 8, 128), (2, 8, 128), (2, n // 8, 8, 128)],
        [SM] + [VM] * 5,
        (idx, vox, rx0, rx1, ry0, ry1),
        limit=1,
    )
    rz1 = swap(vox, "gz", 1, "voxel_z1")
    rz0 = swap(vox, "gz", 0, "voxel_z0")
    re0 = swap(edge, "gx", 0, "corner_x0")
    re1 = swap(edge, "gx", 1, "corner_x1")
    sc, sf = call(
        middle,
        [(n + 4, 24, 128), (n + 2, 24, 128)],
        [VM] * 4,
        (vox, p, a, a2),
        [pltpu.VMEM((n // 8 + 2, 24, 128), F32)],
    )
    gd, gc, _, _ = call(
        partial(adjoint, ends),
        [(n, 16, 128)] * 2 + [(n + 4, 24, 128), (n + 2, 24, 128)],
        [SM] + [VM] * 15,
        (idx, vox, rz0, rz1, re0, re1, p, t, h, a, later, later_z, r1, r2, sc, sf),
        [
            pltpu.VMEM((n, 16, 128), F32),
            pltpu.VMEM((n, 16, 128), F32),
            pltpu.VMEM((5, 2, 24, 128), F32),
            pltpu.SemaphoreType.DMA((6,)),
        ],
        alias={14: 2, 15: 3},
        hbm=2,
    )
    return gd, gc


def solution(mesh):
    spec = P("gx", "gy", "gz")
    return jax.shard_map(
        shards, mesh=mesh, in_specs=(spec,) * 8 + (P(),), out_specs=(spec, spec), check_vma=False
    )
```
